256 devices in a mesh: vel: 32 (over x, z), gx: 8 (over y, core).
Axes of the slice: x: 4, y: 4, z: 8, core: 2. Of those that a mesh axis runs over, the one named last changes fastest.
Arguments:
- distribution: float32 [13824, 128, 128], P('vel', 'gx')
- speeds: float32 [3, 13824], P(None, 'vel'), may hold values from 0.03 to 3, as said below
- weights: float32 [13824], P('vel'), may hold values from 3.616898e-05 to 0.00014467593
- octant: int32 [32], P('vel'), may hold values from 0 to 3, as said below
- inverses: float32 [12, 128, 128], replicated, as said below
- inflow: float32 [13824, 128], P('vel'), may hold values from -6 to 6
- solid_cells: int32 [128, 128], P('gx'), may hold values 0 or 1
Outputs:
- new_distribution: float32 [13824, 128, 128], P('vel', 'gx')
- moment_fields: float32 [8, 128, 128], P(None, 'gx')
The draws below stay inside these ranges and needn't reach their ends.
Inputs may be any that keep to these rules, and one draw needn't show every extreme that they name: `octant`: every value occurs among the shards. `speeds`: all magnitudes are positive. `inverses`: each inverse is lower triangular.
All inputs are finite; a program needn't handle non-finite values. No bound on the sum of `solid_cells` on one device may be relied on, other than what follows from the above.
Results may differ from the reference program's by a relative error of at most 0.0003.
Values sent between devices are 32-bit elements; how exact they have to be, the bound alone decides.
A program may use at most 64 MiB of HBM per device.

```python
import math
import jax
import jax.numpy as jnp
from jax import lax

NY = 128
NCLS = 12
SWEEPS = 2
VEL = 13824
SHARDS = 32
NX = 128


def draw_distribution(key, part):
    base_key, scale_key, noise_key = jax.random.split(key, 3)
    profile = jax.random.normal(base_key, (NX, NY), jnp.float32)
    noise = 0.5 * jax.random.normal(noise_key, (VEL, NX, NY), jnp.float32)
    scales = jnp.exp(jax.random.uniform(scale_key, (VEL, 1, 1), jnp.float32, math.log(0.5), math.log(2.0)))
    return profile[None] * scales + noise


def draw_speeds(key, part):
    stream_key, cross_key = jax.random.split(key)
    lowest = math.log(0.03)
    stream = jnp.exp(jax.random.uniform(stream_key, (1, VEL), jnp.float32, lowest, math.log(3.0)))
    cross = jnp.exp(jax.random.uniform(cross_key, (2, VEL), jnp.float32, math.log(0.1), math.log(3.0)))
    return jnp.concatenate([stream, cross], axis=0)


def draw_octant(key, part):
    return (jax.random.permutation(key, SHARDS) % 4).astype(jnp.int32)


def draw_inverses(key, part):
    diag_key, below_key = jax.random.split(key)
    row_index = jnp.arange(NY)[:, None]
    col_index = jnp.arange(NY)[None, :]
    distance = jnp.maximum(row_index - col_index, 0).astype(jnp.float32)
    below_diag = jax.random.uniform(below_key, (NCLS, NY, NY), jnp.float32, -1.0, 1.0) * 0.15 * jnp.exp(-distance / 8.0)
    below_diag = jnp.where(row_index > col_index, below_diag, 0.0)
    diagonal = jax.random.uniform(diag_key, (NCLS, NY, 1), jnp.float32, 0.5, 0.8)
    return below_diag + jnp.where(row_index == col_index, diagonal, 0.0)


def place_ends(array, key, smallest, high):
    index_at = [jax.random.randint(jax.random.fold_in(key, axis), (), 0, length) for axis, length in enumerate(array.shape)]
    main_axis = array.shape.index(max(array.shape))
    beside = index_at[:main_axis] + [(index_at[main_axis] + 1) % array.shape[main_axis]] + index_at[main_axis + 1:]
    return array.at[tuple(index_at)].set(smallest).at[tuple(beside)].set(high)


def steps_of(rng, dims, shards, smallest, top_value):
    def one(axis_at, blocks):
        steps = jax.random.uniform(jax.random.fold_in(jax.random.fold_in(rng, 6), axis_at), (blocks,), jnp.float32, smallest / len(shards), top_value / len(shards))
        return jnp.repeat(jnp.exp(steps), dims[axis_at] // blocks).reshape((-1,) + (1,) * (len(dims) - axis_at - 1))

    loudness = one(*shards[0])
    for cut in shards[1:]:
        loudness = loudness * one(*cut)
    return loudness


def scatter_about(own_key, shape, scale, limit, cuts=(), kind=jnp.bfloat16):
    values = jax.random.normal(own_key, shape, jnp.float32) * scale
    if len(cuts) > 0:
        values = steps_of(own_key, shape, cuts, -0.22, 0.18) * values
    return jnp.clip(values, min=-limit, max=limit).astype(kind)


def setup_inputs(seed: int = 0) -> dict:
    seeds = jax.random.split(jax.random.key(seed), 8)
    distribution = draw_distribution(jax.random.fold_in(seeds[7], 71), 0)
    speeds = draw_speeds(jax.random.fold_in(seeds[7], 71), 0)
    weights = jnp.clip(jnp.exp(math.log(0.00014467593) - 1.3862944 * jax.random.uniform(seeds[2], (VEL,), jnp.float32) ** steps_of(seeds[2], (VEL,), ((0, 32),), -0.2, 0.2)), 3.616898175096139e-05, 0.00014467593)
    octant = draw_octant(jax.random.fold_in(seeds[7], 71), 0)
    inverses = draw_inverses(jax.random.fold_in(seeds[7], 71), 0)
    inflow = scatter_about(seeds[5], (VEL, NY), 1.0, 6.0, ((0, 32),), jnp.float32)
    solid_cells = place_ends((jax.random.randint(seeds[6], (NX, NY), 0, 64) < 1).astype(jnp.int32), jax.random.fold_in(seeds[6], 1), 0, 1)
    return dict(distribution=distribution, speeds=speeds, weights=weights, octant=octant, inverses=inverses, inflow=inflow, solid_cells=solid_cells)


PRECISE = lax.Precision.HIGHEST
SHAKHOV = 4.0 / 45.0
KNUDSEN_STEP = 0.004
ABSORB = 0.3


def signed_speeds(speed_block, quadrant):
    velocity_count = speed_block.shape[1]
    position = jnp.arange(velocity_count, dtype=jnp.int32)
    sign_x = jnp.where(position < velocity_count // 2, 1.0, -1.0).astype(jnp.float32)
    sign_y = (1 - 2 * (quadrant % 2)).astype(jnp.float32)
    sign_z = (1 - 2 * (quadrant // 2)).astype(jnp.float32)
    return speed_block[0] * sign_x, speed_block[1] * sign_y, speed_block[2] * sign_z


def bases(speed_x, speed_y, speed_z):
    energy = speed_x * speed_x + speed_y * speed_y + speed_z * speed_z
    flux_part = energy - 2.5
    unity = jnp.ones_like(speed_x)
    moment_rows = jnp.stack([unity, speed_x, speed_y, speed_z, energy * (2.0 / 3.0) - 1.0,
                             speed_x * flux_part, speed_y * flux_part, speed_z * flux_part])
    source_rows = jnp.stack([unity, 2.0 * speed_x, 2.0 * speed_y, 2.0 * speed_z, energy - 1.5,
                             SHAKHOV * speed_x * flux_part, SHAKHOV * speed_y * flux_part,
                             SHAKHOV * speed_z * flux_part])
    return moment_rows, source_rows


def reference(distribution, speeds, weights, octant, inverses, inflow, solid_cells):
    shard_count = octant.shape[0]
    velocity_count = distribution.shape[0] // shard_count
    half_count = velocity_count // 2
    classes = inverses.shape[0]
    cells_x = distribution.shape[1]
    cells_y = distribution.shape[2]
    speed_blocks = speeds.reshape(3, shard_count, velocity_count).transpose(1, 0, 2)
    weight_blocks = weights.reshape(shard_count, velocity_count)
    inflow_blocks = inflow.reshape(shard_count, velocity_count, cells_y)
    retained = 1.0 - ABSORB * solid_cells.astype(jnp.float32)
    flipped = inverses[:, ::-1, ::-1]

    def moments(field_blocks):
        def advance(accumulated, inputs):
            shard_field, speed_block, weight_block, quadrant = inputs
            speed_x, speed_y, speed_z = signed_speeds(speed_block, quadrant)
            moment_rows, source_rows = bases(speed_x, speed_y, speed_z)
            flattened = shard_field.reshape(velocity_count, cells_x * cells_y)
            term = jnp.dot(moment_rows * weight_block[None, :], flattened, precision=PRECISE,
                           preferred_element_type=jnp.float32)
            return accumulated + term, None

        start = jnp.zeros((8, cells_x * cells_y), jnp.float32)
        accumulated, _ = lax.scan(advance, start, (field_blocks, speed_blocks, weight_blocks, octant))
        return accumulated

    def sweep_shard(inputs, moment_field):
        speed_block, quadrant, inflow_block = inputs
        speed_x, speed_y, speed_z = signed_speeds(speed_block, quadrant)
        moment_rows, source_rows = bases(speed_x, speed_y, speed_z)
        source = jnp.dot(source_rows.T, moment_field, precision=PRECISE, preferred_element_type=jnp.float32)
        source = source.reshape(2, velocity_count // (2 * classes), classes, cells_x, cells_y)
        operator = jnp.where(quadrant % 2 == 0, inverses, flipped)
        relaxed = jnp.einsum('kyz,srkxz->srkxy', operator, source, precision=PRECISE)
        relaxed = relaxed.reshape(velocity_count, cells_x, cells_y)
        decay_rates = (jnp.abs(speed_x) / (jnp.abs(speed_x) + KNUDSEN_STEP))[:, None]

        def march(rates):
            def advance(previous, columns):
                relaxed_column, kept_column = columns
                updated = rates * kept_column[None, :] * previous + (1.0 - rates) * relaxed_column
                return updated, updated
            return advance

        _, forward_cols = lax.scan(march(decay_rates[:half_count]), inflow_block[:half_count],
                                   (jnp.moveaxis(relaxed[:half_count], 1, 0), retained))
        _, backward_cols = lax.scan(march(decay_rates[half_count:]), inflow_block[half_count:],
                                    (jnp.moveaxis(relaxed[half_count:], 1, 0), retained), reverse=True)
        return jnp.concatenate([jnp.moveaxis(forward_cols, 0, 1), jnp.moveaxis(backward_cols, 0, 1)], axis=0)

    field_blocks = distribution.reshape(shard_count, velocity_count, cells_x, cells_y)
    for sweep_index in range(SWEEPS):
        moment_field = moments(field_blocks)
        field_blocks = lax.map(lambda inputs: sweep_shard(inputs, moment_field),
                               (speed_blocks, octant, inflow_blocks))
    final_moments = moments(field_blocks)
    return field_blocks.reshape(distribution.shape), final_moments.reshape(8, cells_x, cells_y)
```

```python
import functools

import jax
import jax.numpy as jnp
from jax import lax
from jax.experimental import pallas as pl
from jax.experimental.pallas import tpu as pltpu
from jax.sharding import PartitionSpec as P


SHAKHOV = 4.0 / 45.0
KNUDSEN_STEP = 0.004
ABSORB = 0.3
SWEEPS = 2
MESH = pl.DeviceIdType.MESH
F32 = jnp.float32
BF16 = jnp.bfloat16

V = 432
H = 216
HP = 224
NC = 12
NM = 8
XS = 16
T = 32
PLANE = 32
CHIPS = 4


def split(x):
    hi = x.astype(BF16)
    return hi, (x - hi.astype(F32)).astype(BF16)


def dot(a, b):
    return jnp.dot(a, b, preferred_element_type=F32)


def rows_of(ax, ay, az, sx, sy, sz):
    cx, cy, cz = ax * sx, ay * sy, az * sz
    e = cx * cx + cy * cy + cz * cz
    f = e - 2.5
    one = jnp.ones_like(cx)
    phi = [one, cx, cy, cz, e * (2.0 / 3.0) - 1.0, cx * f, cy * f, cz * f]
    psi = [one, 2.0 * cx, 2.0 * cy, 2.0 * cz, e - 1.5, SHAKHOV * cx * f, SHAKHOV * cy * f, SHAKHOV * cz * f]
    return phi, psi


def body(
    dist, speeds, weights, octant, inverses, inflow, solid,
    out_h, out_m,
    dx, spd, wall, wdir, inv, infl, sbuf, part0, part, own, rb1, rb2, mb, mo,
    b3, a3, at, abc, a32, ks, kc, kp, tsc, t2, gs, hloc, mloc, ebuf, esrc, hin,
    dsem, isem, ssend, srecv, rsend, rrecv, gsend, grecv, esend, erecv, osend, orecv, olocal,
):
    vel = lax.axis_index("vel")
    gx = lax.axis_index("gx")
    y = gx // 2
    c = gx % 2
    owner = (vel % 2) == c
    p = jnp.where(c == 0, y, CHIPS - 1 - y)

    def step_of(row, core):
        return jnp.where(core == 0, row, T - 1 - row)

    def remote(src, dst, ss, rs, tv, tg):
        return pltpu.make_async_remote_copy(
            src_ref=src, dst_ref=dst, send_sem=ss, recv_sem=rs, device_id=(tv, tg), device_id_type=MESH
        )

    def send(src, dst, ss, rs, tv, tg):
        here = (tv == vel) & (tg == gx)

        @pl.when(here)
        def _():
            pltpu.make_async_copy(src, dst, rs).start()

        @pl.when(jnp.logical_not(here))
        def _():
            remote(src, dst, ss, rs, tv, tg).start()

    for x in range(XS):
        pltpu.make_async_copy(dist.at[:, x, :], dx.at[x], dsem.at[x]).start()
    inv_copy = pltpu.make_async_copy(inverses, inv, isem.at[0])
    inv_copy.start()
    infl_copy = pltpu.make_async_copy(
        inflow.at[pl.ds(pl.multiple_of(c * H, 8), H)], infl.at[pl.ds(0, H)], isem.at[1]
    )
    infl_copy.start()

    barrier = pltpu.get_barrier_semaphore()

    def greet(i, _):
        tv, tg = i // 2, 2 * y + i % 2

        @pl.when(jnp.logical_not((tv == vel) & (tg == gx)))
        def _():
            pl.semaphore_signal(barrier, inc=1, device_id=(tv, tg), device_id_type=MESH)

        return 0

    lax.fori_loop(0, 2 * PLANE, greet, 0)
    for o in range(1, CHIPS):
        for cc in range(2):
            pl.semaphore_signal(
                barrier, inc=1, device_id=(vel, lax.rem(y + o, CHIPS) * 2 + cc), device_id_type=MESH
            )

    lane = lax.broadcasted_iota(jnp.int32, (1, 512), 1)
    quadrant = octant[0]
    sy = (1 - 2 * lax.rem(quadrant, 2)).astype(F32)
    sz = (1 - 2 * lax.div(quadrant, 2)).astype(F32)
    spd[...] = jnp.zeros_like(spd)
    spd[0:3, 0:V] = speeds[...]
    spd[3:4, 0:V] = weights[...]
    sp = spd[...]
    sx_all = jnp.where(lane < H, 1.0, -1.0).astype(F32)
    phi, _ = rows_of(sp[0:1], sp[1:2], sp[2:3], sx_all, sy, sz)
    for m in range(NM):
        spd[m : m + 1, :] = phi[m] * sp[3:4]
    hi, lo = split(spd[...])
    wall[...] = jnp.concatenate([hi.astype(F32), lo.astype(F32)], axis=0).astype(BF16)

    for x in range(XS):
        pltpu.make_async_copy(dist.at[:, x, :], dx.at[x], dsem.at[x]).wait()
        hi, lo = split(dx[x])
        r = dot(wall[:, 0:V], jnp.concatenate([hi, lo], axis=1))
        part0[x] = r[0:8, 0:128] + r[8:16, 0:128] + r[0:8, 128:256] + r[8:16, 128:256]

    pl.semaphore_wait(barrier, 2 * PLANE - 1 + 2 * (CHIPS - 1))

    def rs1(i, _):
        i = lax.rem(i + vel, XS)
        row = XS * c + i
        send(part0.at[i], rb1.at[vel], rsend.at[0], rrecv.at[0], row, 2 * y + row % 2)
        return 0

    lax.fori_loop(0, XS, rs1, 0)

    for o in range(1, 2 * CHIPS):
        remote(solid, sbuf.at[gx], ssend, srecv, vel, lax.rem(gx + o, 2 * CHIPS)).start()
    pltpu.make_async_copy(solid, sbuf.at[gx], srecv).start()

    sp = jnp.where(c == 0, sp, pltpu.roll(sp, 512 - H, 1))
    sp = jnp.where(lane < H, sp, 0.0)
    sp = sp[:, 0:256]
    live = (lane < H).astype(F32)[:, 0:256]
    sx = (1 - 2 * c).astype(F32)
    phi, psi = rows_of(sp[0:1], sp[1:2], sp[2:3], sx, sy, sz)
    rate = sp[0:1] / (sp[0:1] + KNUDSEN_STEP)
    for m in range(NM):
        spd[m : m + 1, 0:256] = phi[m] * sp[3:4]
        spd[m : m + 1, 256:512] = psi[m] * ((1.0 - rate) * live)
    wd = spd[:, 0:256]
    ps = spd[:, 256:512]
    hi, lo = split(wd)
    wdir[...] = jnp.concatenate([hi.astype(F32), lo.astype(F32)], axis=0).astype(BF16)
    cls = lax.rem(lax.broadcasted_iota(jnp.int32, (8, 256), 1), NC)
    hi, lo = split(ps)
    hi, lo = hi.astype(F32), lo.astype(F32)
    for k in range(NC):
        at[8 * k : 8 * k + 8] = jnp.where(cls == k, hi, 0.0)
        at[96 + 8 * k : 104 + 8 * k] = jnp.where(cls == k, lo, 0.0)
        at[192 + 8 * k : 200 + 8 * k] = jnp.where(cls == k, hi, 0.0)
    at[288:384] = jnp.zeros((96, 256), F32)
    a3[...] = at[...].T[0:HP].astype(BF16)
    abc[...] = jnp.broadcast_to(rate, (128, 256)).T[0:HP]
    pw = abc[...]
    for _ in range(5):
        pw = pw * pw
    a32[...] = pw
    infl[H:HP] = jnp.zeros((HP - H, 128), F32)
    infl_copy.wait()

    def powers(t, cur):
        cur = cur * rate
        tsc[t] = cur
        return cur

    lax.fori_loop(0, T, powers, wd)
    hi, lo = split(tsc[...].reshape(T * NM, 256))
    t2[0 : T * NM] = hi
    t2[T * NM : 2 * T * NM] = lo

    def gather(rb, n, k, wait):
        @pl.when(owner)
        def _():
            full = rb.at[pl.ds(0, n)]
            remote(full, full, rsend.at[k], rrecv.at[k], vel, gx).wait_recv()
            own[k] = jnp.sum(rb[...].reshape(n // 8, 8, NM, 128), axis=0).sum(axis=0)

    gather(rb1, PLANE, 0, None)

    def spread(k, dst):
        @pl.when(owner)
        def _():
            def one(i, _):
                j = lax.rem(i + 2 * vel + c + 1, 2 * PLANE)
                tv, tc = j // 2, j % 2
                send(own.at[k], dst.at[step_of(vel, tc)], gsend.at[k], grecv.at[k], tv, 2 * y + tc)
                return 0

            lax.fori_loop(0, 2 * PLANE, one, 0)

    spread(0, mb.at[0])

    inv_copy.wait()
    ii = lax.broadcasted_iota(jnp.int32, (128, 128), 0)
    jj = lax.broadcasted_iota(jnp.int32, (128, 128), 1)
    perm = (ii == jnp.where(lax.rem(quadrant, 2) == 0, jj, 127 - jj)).astype(F32).astype(BF16)
    for n in range(NC // 2):
        parts = split(inv[2 * n : 2 * n + 2].reshape(256, 128))
        for q, w in enumerate(parts):
            u = lax.dot_general(perm, w, (((1,), (1,)), ((), ())), preferred_element_type=F32)
            u = jnp.concatenate([u[:, 0:128], u[:, 128:256]], axis=0).astype(BF16)
            v = dot(u, perm).astype(BF16)
            v = jnp.concatenate([v[0:128], v[128:256]], axis=1)
            cols = slice(256 * n, 256 * n + 256)
            if q == 0:
                b3[0:128, cols] = v
                b3[128:256, cols] = v
            else:
                b3[256:384, cols] = v

    remote(sbuf, sbuf, ssend, srecv, vel, gx).wait_recv()
    for chip in range(CHIPS):
        keep = 1.0 - ABSORB * sbuf[2 * chip : 2 * chip + 2].astype(F32).reshape(4, 8, 128)
        keep = (keep[0] * keep[1]) * (keep[2] * keep[3])
        for s in (4, 2, 1):
            keep = keep * pltpu.roll(keep, s, 0)
        kp[chip] = keep

    def cells(t, cur):
        x = step_of(t, c)
        keep = 1.0 - ABSORB * sbuf[2 * y + x // XS, pl.ds(x % XS, 1), :].astype(F32)
        keep = jnp.broadcast_to(keep, (8, 128))
        cur = cur * keep
        ks[t] = keep
        kc[t] = cur
        return cur

    lax.fori_loop(0, T, cells, jnp.ones((8, 128), F32))

    for s in range(SWEEPS):
        remote(mb.at[s], mb.at[s], gsend.at[s], grecv.at[s], vel, gx).wait_recv()
        hi, lo = split(mb[s].reshape(T * NM, 128))
        l3 = jnp.concatenate([hi, lo, hi], axis=1)
        for n in range(NC // 2):
            g = dot(l3, b3[:, 256 * n : 256 * n + 256]).reshape(T, NM, 256)
            hi, lo = split(jnp.concatenate([g[:, :, 0:128], g[:, :, 128:256]], axis=1))
            gs[:, 16 * n : 16 * n + 16, :] = hi
            gs[:, 96 + 16 * n : 112 + 16 * n, :] = hi
            gs[:, 192 + 16 * n : 208 + 16 * n, :] = lo

        def march(u, h):
            t = 2 * u
            r = dot(a3[:, 0:288], jnp.concatenate([gs[t], gs[t + 1]], axis=1))
            a = abc[...].reshape(HP // 8, 8, 128)
            for d in range(2):
                h = h * (a * ks[t + d][None]) + r[:, 128 * d : 128 * d + 128].reshape(HP // 8, 8, 128)
                hloc[t + d] = h.reshape(HP, 128)
            return h

        h = lax.fori_loop(0, T // 2, march, jnp.zeros((HP // 8, 8, 128), F32), unroll=2)
        esrc[s] = h.reshape(HP, 128)

        for q in (3, 2, 1):

            @pl.when(q > p)
            def _():
                ty = jnp.where(c == 0, q, CHIPS - 1 - q)
                remote(esrc.at[s], ebuf.at[s, p], esend.at[s, q - 1], erecv.at[s, p], vel, 2 * ty + c).start()

        def local_moments(u, _):
            t = 2 * u
            hi, lo = split(jnp.concatenate([hloc[t], hloc[t + 1]], axis=1))
            r = dot(wdir[:, 0:HP], hi) + dot(wdir[:, 0:HP], lo)
            r = r[0:8] + r[8:16]
            mloc[t] = r[:, 0:128]
            mloc[t + 1] = r[:, 128:256]
            return 0

        lax.fori_loop(0, T // 2, local_moments, 0, unroll=2)

        hin[...] = infl[...]
        for q in range(CHIPS - 1):

            @pl.when(q < p)
            def _():
                remote(esrc.at[s], ebuf.at[s, q], esend.at[s, 0], erecv.at[s, q], vel, gx).wait_recv()
                k = kp[jnp.where(c == 0, q, CHIPS - 1 - q)]
                span = a32[...].reshape(HP // 8, 8, 128) * k[None]
                now = hin[...].reshape(HP // 8, 8, 128) * span + ebuf[s, q].reshape(HP // 8, 8, 128)
                hin[...] = now.reshape(HP, 128)

        hi, lo = split(hin[...])
        r = dot(t2[:, 0:HP], jnp.concatenate([hi, lo], axis=1))
        n = T * NM
        r = (r[0:n, 0:128] + r[n : 2 * n, 0:128]) + (r[0:n, 128:256] + r[n : 2 * n, 128:256])
        part[s] = mloc[...] + kc[...] * r.reshape(T, NM, 128)

        def rs(i, _):
            row = lax.rem(i + vel, T)
            send(
                part.at[s, step_of(row, c)], rb2.at[s, 2 * vel + c], rsend.at[s + 1], rrecv.at[s + 1],
                row, 2 * y + row % 2,
            )
            return 0

        lax.fori_loop(0, T, rs, 0)

        if s == SWEEPS - 1:
            def finish(t, h):
                a = abc[...].reshape(HP // 8, 8, 128)
                h = h * (a * ks[t][None])
                hloc[t] = (hloc[t].reshape(HP // 8, 8, 128) + h).reshape(HP, 128)
                return h

            first = pl.multiple_of(c * H, 8)

            def far(t, h):
                h = finish(t, h)
                x = jnp.where(c == 0, t - XS, T - 1 - t)
                remote(
                    hloc.at[t, pl.ds(0, H)], out_h.at[pl.ds(first, H), x, :], osend, orecv, vel, 2 * y + 1 - c
                ).start()
                return h

            def near(t, h):
                h = finish(t, h)
                x = jnp.where(c == 0, t, XS - 1 - t)
                pltpu.make_async_copy(hloc.at[t, pl.ds(0, H)], out_h.at[pl.ds(first, H), x, :], olocal).start()
                return h

            h = lax.fori_loop(0, XS, near, hin[...].reshape(HP // 8, 8, 128))
            lax.fori_loop(XS, T, far, h)

        gather(rb2.at[s], 2 * PLANE, s + 1, None)
        if s < SWEEPS - 1:
            spread(s + 1, mb.at[s + 1])

    last = SWEEPS
    section = vel // XS

    @pl.when(owner)
    def _():
        def one(i, _):
            tv = lax.rem(i + vel + 1, PLANE)
            send(own.at[last], mo.at[vel % XS], gsend.at[last], grecv.at[last], tv, 2 * y + section)
            return 0

        lax.fori_loop(0, PLANE, one, 0)

    remote(mo, mo, gsend.at[last], grecv.at[last], vel, gx).wait_recv()
    for x in range(XS):
        out_m[:, x, :] = mo[x]

    for o in range(1, 2 * CHIPS):
        remote(solid, sbuf.at[gx], ssend, srecv, vel, gx).wait_send()
    mine = owner & (section == c)

    def drain(buf, n, less, sem):
        @pl.when(less)
        def _():
            remote(buf.at[pl.ds(0, n - 1)], buf.at[pl.ds(0, n - 1)], sem, sem, vel, gx).wait_send()

        @pl.when(jnp.logical_not(less))
        def _():
            remote(buf.at[pl.ds(0, n)], buf.at[pl.ds(0, n)], sem, sem, vel, gx).wait_send()

    drain(part0, XS, mine, rsend.at[0])
    for s in range(SWEEPS):
        drain(part.at[s], T, owner, rsend.at[s + 1])
        for q in (3, 2, 1):

            @pl.when(q > p)
            def _():
                remote(esrc.at[s], esrc.at[s], esend.at[s, q - 1], esend.at[s, q - 1], vel, gx).wait_send()

    @pl.when(owner)
    def _():
        for k in range(SWEEPS):
            few = rb2.at[0, pl.ds(0, 2 * PLANE - 1)]
            remote(few, few, gsend.at[k], gsend.at[k], vel, gx).wait_send()
        drain(rb2.at[0], PLANE, section == c, gsend.at[last])

    half = hloc.at[pl.ds(0, XS), pl.ds(0, H)]
    remote(half, half, osend, orecv, vel, gx).wait()
    pltpu.make_async_copy(half, half, olocal).wait()


def per_device(distribution, speeds, weights, octant, inverses, inflow, solid_cells):
    dma = pltpu.SemaphoreType.DMA
    vm = pltpu.VMEM
    scratch = [
        vm((XS, V, 128), F32), vm((8, 512), F32), vm((16, 512), BF16), vm((16, 256), BF16),
        vm((NC, 128, 128), F32), vm((HP, 128), F32), vm((2 * CHIPS, XS, 128), jnp.int32),
        vm((XS, NM, 128), F32), vm((SWEEPS, T, NM, 128), F32), vm((SWEEPS + 1, NM, 128), F32),
        vm((PLANE, NM, 128), F32), vm((SWEEPS, 2 * PLANE, NM, 128), F32), vm((SWEEPS, T, NM, 128), F32),
        vm((XS, NM, 128), F32),
        vm((384, NC * 128), BF16), vm((HP, 384), BF16), vm((384, 256), F32), vm((HP, 128), F32),
        vm((HP, 128), F32), vm((T, 8, 128), F32), vm((T, 8, 128), F32), vm((CHIPS, 8, 128), F32),
        vm((T, 8, 256), F32), vm((2 * T * NM, 256), BF16), vm((T, 288, 128), BF16), vm((T, HP, 128), F32),
        vm((T, NM, 128), F32), vm((SWEEPS, CHIPS - 1, HP, 128), F32), vm((SWEEPS, HP, 128), F32),
        vm((HP, 128), F32),
        dma((XS,)), dma((2,)), dma, dma, dma((SWEEPS + 1,)), dma((SWEEPS + 1,)), dma((SWEEPS + 1,)),
        dma((SWEEPS + 1,)), dma((SWEEPS, CHIPS - 1)), dma((SWEEPS, CHIPS - 1)), dma, dma, dma,
    ]
    hbm = pl.BlockSpec(memory_space=pl.ANY)
    vmem = pl.BlockSpec(memory_space=pltpu.VMEM)
    return pl.pallas_call(
        body,
        out_shape=(
            jax.ShapeDtypeStruct((V, XS, 128), F32),
            jax.ShapeDtypeStruct((NM, XS, 128), F32),
        ),
        in_specs=[hbm, vmem, vmem, pl.BlockSpec(memory_space=pltpu.SMEM), hbm, hbm, hbm],
        out_specs=(hbm, vmem),
        scratch_shapes=scratch,
        name="solve",
        compiler_params=pltpu.CompilerParams(
            collective_id=0, has_side_effects=True, vmem_limit_bytes=48 * 2**20
        ),
    )(distribution, speeds, weights.reshape(1, V), octant, inverses, inflow, solid_cells)


def solution(mesh):
    in_specs = (
        P("vel", "gx", None),
        P(None, "vel"),
        P("vel"),
        P("vel"),
        P(),
        P("vel", None),
        P("gx", None),
    )
    out_specs = (P("vel", "gx", None), P(None, "gx", None))
    return jax.shard_map(
        per_device, mesh=mesh, in_specs=in_specs, out_specs=out_specs, check_vma=False
    )
```

```python
import functools

import jax
import jax.numpy as jnp
from jax import lax
from jax.experimental import pallas as pl
from jax.experimental.pallas import tpu as pltpu
from jax.sharding import PartitionSpec as P


SHAKHOV = 4.0 / 45.0
KNUDSEN_STEP = 0.004
ABSORB = 0.3
SWEEPS = 2
MESH = pl.DeviceIdType.MESH
F32 = jnp.float32
BF16 = jnp.bfloat16

V = 432
H = 216
HP = 224
NC = 12
NM = 8
XS = 16
T = 32
PLANE = 32
ZX = 4
ZS = 8
CHIPS = 4


def split(x):
    hi = x.astype(BF16)
    return hi, (x - hi.astype(F32)).astype(BF16)


def dot(a, b):
    return jnp.dot(a, b, preferred_element_type=F32)


def rows_of(ax, ay, az, sx, sy, sz):
    cx, cy, cz = ax * sx, ay * sy, az * sz
    e = cx * cx + cy * cy + cz * cz
    f = e - 2.5
    one = jnp.ones_like(cx)
    phi = [one, cx, cy, cz, e * (2.0 / 3.0) - 1.0, cx * f, cy * f, cz * f]
    psi = [one, 2.0 * cx, 2.0 * cy, 2.0 * cz, e - 1.5, SHAKHOV * cx * f, SHAKHOV * cy * f, SHAKHOV * cz * f]
    return phi, psi


def body(
    dist, speeds_in, weights_in, octant, inverses, inflow, solid,
    out_h, out_m,
    speeds, weights, dx, spd, wall, wdir, inv, infl, sbuf, part0, part, own, rb1, rb2, mb, mo,
    b3, a3, at, abc, a32, ks, kc, kp, tsc, t2, gs, hloc, mloc, ebuf, esrc, hin, et, ec, kr,
    dsem, isem, ssend, srecv, rsend, rrecv, gsend, grecv, esend, erecv, osend, orecv, olocal,
):
    vel = lax.axis_index("vel")
    gx = lax.axis_index("gx")
    y = gx // 2
    c = gx % 2
    xi = vel // ZS
    zi = vel % ZS
    owner = (vel % 2) == c
    p = jnp.where(c == 0, y, CHIPS - 1 - y)

    def step_of(row, core):
        return jnp.where(core == 0, row, T - 1 - row)

    def remote(src, dst, ss, rs, tv, tg):
        return pltpu.make_async_remote_copy(
            src_ref=src, dst_ref=dst, send_sem=ss, recv_sem=rs, device_id=(tv, tg), device_id_type=MESH
        )

    def send(src, dst, ss, rs, tv, tg, maybe=True):
        if not maybe:
            remote(src, dst, ss, rs, tv, tg).start()
            return
        here = (tv == vel) & (tg == gx)

        @pl.when(here)
        def _():
            pltpu.make_async_copy(src, dst, rs).start()

        @pl.when(jnp.logical_not(here))
        def _():
            remote(src, dst, ss, rs, tv, tg).start()

    small = [
        pltpu.make_async_copy(speeds_in, speeds, isem.at[2]),
        pltpu.make_async_copy(weights_in, weights, isem.at[3]),
    ]
    for copy in small:
        copy.start()
    for x in range(XS):
        pltpu.make_async_copy(dist.at[:, x, :], dx.at[x], dsem.at[x]).start()
    inv_copy = pltpu.make_async_copy(inverses, inv, isem.at[0])
    inv_copy.start()
    infl_copy = pltpu.make_async_copy(
        inflow.at[pl.ds(pl.multiple_of(c * H, 8), H)], infl.at[pl.ds(0, H)], isem.at[1]
    )
    infl_copy.start()

    barrier = pltpu.get_barrier_semaphore()

    def around(i):
        return lax.rem(zi + ZS // 2 + ((i + 1) // 2) * (2 * (i % 2) - 1) + ZS, ZS)

    def greet(i, _):
        tz = around(i)
        for o in (2, 1, 3, 0):
            tv = lax.rem(xi + o, ZX) * ZS + tz
            for cc in range(2):
                if o:
                    pl.semaphore_signal(barrier, inc=1, device_id=(tv, 2 * y + cc), device_id_type=MESH)
                    continue

                @pl.when(jnp.logical_not((tv == vel) & (cc == c)))
                def _():
                    pl.semaphore_signal(barrier, inc=1, device_id=(tv, 2 * y + cc), device_id_type=MESH)

        return 0

    lax.fori_loop(0, ZS, greet, 0)
    for o in range(1, CHIPS):
        for cc in range(2):
            pl.semaphore_signal(
                barrier, inc=1, device_id=(vel, lax.rem(y + o, CHIPS) * 2 + cc), device_id_type=MESH
            )

    lane = lax.broadcasted_iota(jnp.int32, (1, 512), 1)
    for copy in small:
        copy.wait()
    quadrant = octant[0]
    sy = (1 - 2 * lax.rem(quadrant, 2)).astype(F32)
    sz = (1 - 2 * lax.div(quadrant, 2)).astype(F32)
    spd[...] = jnp.zeros_like(spd)
    spd[0:3, 0:V] = speeds[...]
    spd[3:4, 0:V] = weights[...]
    sp = spd[...]
    sx_all = jnp.where(lane < H, 1.0, -1.0).astype(F32)
    phi, _ = rows_of(sp[0:1], sp[1:2], sp[2:3], sx_all, sy, sz)
    for m in range(NM):
        spd[m : m + 1, :] = phi[m] * sp[3:4]
    hi, lo = split(spd[...])
    wall[...] = jnp.concatenate([hi.astype(F32), lo.astype(F32)], axis=0).astype(BF16)

    for x in range(XS):
        pltpu.make_async_copy(dist.at[:, x, :], dx.at[x], dsem.at[x]).wait()
        hi, lo = split(dx[x])
        r = dot(wall[:, 0:V], jnp.concatenate([hi, lo], axis=1))
        part0[x] = r[0:8, 0:128] + r[8:16, 0:128] + r[0:8, 128:256] + r[8:16, 128:256]

    pl.semaphore_wait(barrier, 2 * PLANE - 1 + 2 * (CHIPS - 1))

    def rs1(i, _):
        tz = around(i)
        for o in range(2):
            row = (2 * c + o) * ZS + tz
            send(part0.at[o * ZS + tz], rb1.at[vel], rsend.at[0], rrecv.at[0], row, 2 * y + tz % 2)
        return 0

    lax.fori_loop(0, ZS, rs1, 0)

    for o in range(1, 2 * CHIPS):
        remote(solid, sbuf.at[gx], ssend, srecv, vel, lax.rem(gx + o, 2 * CHIPS)).start()
    pltpu.make_async_copy(solid, sbuf.at[gx], srecv).start()

    sp = jnp.where(c == 0, sp, pltpu.roll(sp, 512 - H, 1))
    sp = jnp.where(lane < H, sp, 0.0)
    sp = sp[:, 0:256]
    live = (lane < H).astype(F32)[:, 0:256]
    sx = (1 - 2 * c).astype(F32)
    phi, psi = rows_of(sp[0:1], sp[1:2], sp[2:3], sx, sy, sz)
    rate = sp[0:1] / (sp[0:1] + KNUDSEN_STEP)
    for m in range(NM):
        spd[m : m + 1, 0:256] = phi[m] * sp[3:4]
        spd[m : m + 1, 256:512] = psi[m] * ((1.0 - rate) * live)
    wd = spd[:, 0:256]
    ps = spd[:, 256:512]
    hi, lo = split(wd)
    wdir[...] = jnp.concatenate([hi.astype(F32), lo.astype(F32)], axis=0).astype(BF16)
    cls = lax.rem(lax.broadcasted_iota(jnp.int32, (8, 256), 1), NC)
    hi, lo = split(ps)
    hi, lo = hi.astype(F32), lo.astype(F32)
    for k in range(NC):
        at[8 * k : 8 * k + 8] = jnp.where(cls == k, hi, 0.0)
        at[96 + 8 * k : 104 + 8 * k] = jnp.where(cls == k, lo, 0.0)
        at[192 + 8 * k : 200 + 8 * k] = jnp.where(cls == k, hi, 0.0)
    at[288:384] = jnp.zeros((96, 256), F32)
    a3[...] = at[...].T[0:HP].astype(BF16)
    abc[...] = jnp.broadcast_to(rate, (128, 256)).T[0:HP]
    pw = abc[...]
    for _ in range(5):
        pw = pw * pw
    a32[...] = pw
    infl[H:HP] = jnp.zeros((HP - H, 128), F32)
    infl_copy.wait()

    def powers(t, cur):
        cur = cur * rate
        tsc[t] = cur
        return cur

    lax.fori_loop(0, T, powers, wd)
    hi, lo = split(tsc[...].reshape(T * NM, 256))
    t2[0 : T * NM] = hi
    t2[T * NM : 2 * T * NM] = lo

    def remains(t, cur):
        tsc[T - 1 - t] = cur
        return cur * rate

    lax.fori_loop(0, T, remains, ps)
    late = tsc[...].reshape(T * NM, 256).T
    for d in range(2):
        et[d, 0:256] = late[:, 128 * d : 128 * d + 128]
        et[d, 256:288] = jnp.zeros((32, 128), F32)
    for k in range(NC):
        hi, lo = split(jnp.concatenate([et[d, pl.ds(k, 24, stride=NC), :] for d in range(2)], axis=1))
        ec[k] = jnp.concatenate([hi.astype(F32), lo.astype(F32)], axis=0).astype(BF16)

    def gather(rb, n, k, wait):
        @pl.when(owner)
        def _():
            full = rb.at[pl.ds(0, n)]
            remote(full, full, rsend.at[k], rrecv.at[k], vel, gx).wait_recv()
            own[k] = jnp.sum(rb[...].reshape(n // 8, 8, NM, 128), axis=0).sum(axis=0)

    gather(rb1, PLANE, 0, None)

    def spread(k, dst):
        @pl.when(owner)
        def _():
            def one(i, _):
                tz = around(i)
                for o in (2, 1, 3, 0):
                    tv = lax.rem(xi + o, ZX) * ZS + tz
                    for tc in range(2):
                        at_row = vel if tc == 0 else T - 1 - vel
                        send(own.at[k], dst.at[at_row], gsend.at[k], grecv.at[k], tv, 2 * y + tc, o == 0)
                return 0

            lax.fori_loop(0, ZS, one, 0)

    spread(0, mb.at[0])

    inv_copy.wait()
    ii = lax.broadcasted_iota(jnp.int32, (128, 128), 0)
    jj = lax.broadcasted_iota(jnp.int32, (128, 128), 1)
    perm = (ii == jnp.where(lax.rem(quadrant, 2) == 0, jj, 127 - jj)).astype(F32).astype(BF16)
    for n in range(NC // 2):
        parts = split(inv[2 * n : 2 * n + 2].reshape(256, 128))
        for q, w in enumerate(parts):
            u = lax.dot_general(perm, w, (((1,), (1,)), ((), ())), preferred_element_type=F32)
            u = jnp.concatenate([u[:, 0:128], u[:, 128:256]], axis=0).astype(BF16)
            v = dot(u, perm).astype(BF16)
            v = jnp.concatenate([v[0:128], v[128:256]], axis=1)
            cols = slice(256 * n, 256 * n + 256)
            if q == 0:
                b3[0:128, cols] = v
                b3[128:256, cols] = v
            else:
                b3[256:384, cols] = v

    remote(sbuf, sbuf, ssend, srecv, vel, gx).wait_recv()
    for chip in range(CHIPS):
        keep = 1.0 - ABSORB * sbuf[2 * chip : 2 * chip + 2].astype(F32).reshape(4, 8, 128)
        keep = (keep[0] * keep[1]) * (keep[2] * keep[3])
        for s in (4, 2, 1):
            keep = keep * pltpu.roll(keep, s, 0)
        kp[chip] = keep

    def cells(t, cur):
        x = step_of(t, c)
        keep = 1.0 - ABSORB * sbuf[2 * y + x // XS, pl.ds(x % XS, 1), :].astype(F32)
        keep = jnp.broadcast_to(keep, (8, 128))
        cur = cur * keep
        ks[t] = keep
        kc[t] = cur
        return cur

    lax.fori_loop(0, T, cells, jnp.ones((8, 128), F32))

    def left(t, cur):
        kr[T - 1 - t] = cur
        return cur * ks[T - 1 - t]

    lax.fori_loop(0, T, left, jnp.ones((8, 128), F32))
    for s in range(SWEEPS):
        esrc[s, H:HP] = jnp.zeros((HP - H, 128), F32)

    for s in range(SWEEPS):
        remote(mb.at[s], mb.at[s], gsend.at[s], grecv.at[s], vel, gx).wait_recv()
        hi, lo = split(mb[s].reshape(T * NM, 128))
        l3 = jnp.concatenate([hi, lo, hi], axis=1)
        for n in range(NC // 2):
            g = dot(l3, b3[:, 256 * n : 256 * n + 256]).reshape(T, NM, 256)
            gs[:, 16 * n : 16 * n + 16, :] = jnp.concatenate([g[:, :, 0:128], g[:, :, 128:256]], axis=1)
            for d in range(2):
                hi, lo = split((g[:, :, 128 * d : 128 * d + 128] * kr[...]).reshape(T * NM, 128))
                r = dot(ec[2 * n + d], jnp.concatenate([hi, lo], axis=1))
                r = r[0:24, 0:128] + r[24:48, 0:128] + r[0:24, 128:256]
                esrc[s, pl.ds(2 * n + d, H // NC, stride=NC), :] = r[0 : H // NC]

        for q in (3, 2, 1):

            @pl.when(q > p)
            def _():
                ty = jnp.where(c == 0, q, CHIPS - 1 - q)
                remote(esrc.at[s], ebuf.at[s, p], esend.at[s, q - 1], erecv.at[s, p], vel, 2 * ty + c).start()

        def march(u, h):
            t = 2 * u
            hi, lo = split(jnp.concatenate([gs[t], gs[t + 1]], axis=1))
            r = dot(a3[:, 0:288], jnp.concatenate([hi, hi, lo], axis=0))
            a = abc[...].reshape(HP // 8, 8, 128)
            for d in range(2):
                h = h * (a * ks[t + d][None]) + r[:, 128 * d : 128 * d + 128].reshape(HP // 8, 8, 128)
                hloc[t + d] = h.reshape(HP, 128)
            return h

        lax.fori_loop(0, T // 2, march, jnp.zeros((HP // 8, 8, 128), F32), unroll=2)

        def local_moments(u, _):
            t = 2 * u
            hi, lo = split(jnp.concatenate([hloc[t], hloc[t + 1]], axis=1))
            r = dot(wdir[:, 0:HP], hi) + dot(wdir[:, 0:HP], lo)
            r = r[0:8] + r[8:16]
            mloc[t] = r[:, 0:128]
            mloc[t + 1] = r[:, 128:256]
            return 0

        lax.fori_loop(0, T // 2, local_moments, 0, unroll=2)

        hin[...] = infl[...]
        for q in range(CHIPS - 1):

            @pl.when(q < p)
            def _():
                remote(esrc.at[s], ebuf.at[s, q], esend.at[s, 0], erecv.at[s, q], vel, gx).wait_recv()
                k = kp[jnp.where(c == 0, q, CHIPS - 1 - q)]
                span = a32[...].reshape(HP // 8, 8, 128) * k[None]
                now = hin[...].reshape(HP // 8, 8, 128) * span + ebuf[s, q].reshape(HP // 8, 8, 128)
                hin[...] = now.reshape(HP, 128)

        hi, lo = split(hin[...])
        r = dot(t2[:, 0:HP], jnp.concatenate([hi, lo], axis=1))
        n = T * NM
        r = (r[0:n, 0:128] + r[n : 2 * n, 0:128]) + (r[0:n, 128:256] + r[n : 2 * n, 128:256])
        part[s] = mloc[...] + kc[...] * r.reshape(T, NM, 128)

        def rs(i, _):
            tz = around(i)
            for o in (2, 1, 3, 0):
                row = lax.rem(xi + o, ZX) * ZS + tz
                send(
                    part.at[s, step_of(row, c)], rb2.at[s, 2 * vel + c], rsend.at[s + 1], rrecv.at[s + 1],
                    row, 2 * y + tz % 2, o == 0,
                )
            return 0

        lax.fori_loop(0, ZS, rs, 0)

        if s == SWEEPS - 1:
            def finish(t, h):
                a = abc[...].reshape(HP // 8, 8, 128)
                h = h * (a * ks[t][None])
                hloc[t] = (hloc[t].reshape(HP // 8, 8, 128) + h).reshape(HP, 128)
                return h

            first = pl.multiple_of(c * H, 8)

            def far(t, h):
                h = finish(t, h)
                x = jnp.where(c == 0, t - XS, T - 1 - t)
                remote(
                    hloc.at[t, pl.ds(0, H)], out_h.at[pl.ds(first, H), x, :], osend, orecv, vel, 2 * y + 1 - c
                ).start()
                return h

            def near(t, h):
                h = finish(t, h)
                x = jnp.where(c == 0, t, XS - 1 - t)
                pltpu.make_async_copy(hloc.at[t, pl.ds(0, H)], out_h.at[pl.ds(first, H), x, :], olocal).start()
                return h

            h = lax.fori_loop(0, XS, near, hin[...].reshape(HP // 8, 8, 128))
            lax.fori_loop(XS, T, far, h)

        gather(rb2.at[s], 2 * PLANE, s + 1, None)
        if s < SWEEPS - 1:
            spread(s + 1, mb.at[s + 1])

    last = SWEEPS
    section = vel // XS

    @pl.when(owner)
    def _():
        def one(i, _):
            tz = around(i)
            for o in (2, 1, 3, 0):
                tv = lax.rem(xi + o, ZX) * ZS + tz
                send(own.at[last], mo.at[vel % XS], gsend.at[last], grecv.at[last], tv, 2 * y + section, o == 0)
            return 0

        lax.fori_loop(0, ZS, one, 0)

    remote(mo, mo, gsend.at[last], grecv.at[last], vel, gx).wait_recv()
    for x in range(XS):
        out_m[:, x, :] = mo[x]

    for o in range(1, 2 * CHIPS):
        remote(solid, sbuf.at[gx], ssend, srecv, vel, gx).wait_send()
    mine = owner & (section == c)

    def drain(buf, n, less, sem):
        @pl.when(less)
        def _():
            remote(buf.at[pl.ds(0, n - 1)], buf.at[pl.ds(0, n - 1)], sem, sem, vel, gx).wait_send()

        @pl.when(jnp.logical_not(less))
        def _():
            remote(buf.at[pl.ds(0, n)], buf.at[pl.ds(0, n)], sem, sem, vel, gx).wait_send()

    drain(part0, XS, mine, rsend.at[0])
    for s in range(SWEEPS):
        drain(part.at[s], T, owner, rsend.at[s + 1])
        for q in (3, 2, 1):

            @pl.when(q > p)
            def _():
                remote(esrc.at[s], esrc.at[s], esend.at[s, q - 1], esend.at[s, q - 1], vel, gx).wait_send()

    @pl.when(owner)
    def _():
        for k in range(SWEEPS):
            few = rb2.at[0, pl.ds(0, 2 * PLANE - 1)]
            remote(few, few, gsend.at[k], gsend.at[k], vel, gx).wait_send()
        drain(rb2.at[0], PLANE, section == c, gsend.at[last])

    half = hloc.at[pl.ds(0, XS), pl.ds(0, H)]
    remote(half, half, osend, orecv, vel, gx).wait()
    pltpu.make_async_copy(half, half, olocal).wait()


def per_device(distribution, speeds, weights, octant, inverses, inflow, solid_cells):
    dma = pltpu.SemaphoreType.DMA
    vm = pltpu.VMEM
    scratch = [
        vm((3, V), F32), vm((1, V), F32),
        vm((XS, V, 128), F32), vm((8, 512), F32), vm((16, 512), BF16), vm((16, 256), BF16),
        vm((NC, 128, 128), F32), vm((HP, 128), F32), vm((2 * CHIPS, XS, 128), jnp.int32),
        vm((XS, NM, 128), F32), vm((SWEEPS, T, NM, 128), F32), vm((SWEEPS + 1, NM, 128), F32),
        vm((PLANE, NM, 128), F32), vm((SWEEPS, 2 * PLANE, NM, 128), F32), vm((SWEEPS, T, NM, 128), F32),
        vm((XS, NM, 128), F32),
        vm((384, NC * 128), BF16), vm((HP, 384), BF16), vm((384, 256), F32), vm((HP, 128), F32),
        vm((HP, 128), F32), vm((T, 8, 128), F32), vm((T, 8, 128), F32), vm((CHIPS, 8, 128), F32),
        vm((T, 8, 256), F32), vm((2 * T * NM, 256), BF16), vm((T, 96, 128), F32), vm((T, HP, 128), F32),
        vm((T, NM, 128), F32), vm((SWEEPS, CHIPS - 1, HP, 128), F32), vm((SWEEPS, HP, 128), F32),
        vm((HP, 128), F32), vm((2, 288, 128), F32), vm((NC, 48, 256), BF16), vm((T, 8, 128), F32),
        dma((XS,)), dma((4,)), dma, dma, dma((SWEEPS + 1,)), dma((SWEEPS + 1,)), dma((SWEEPS + 1,)),
        dma((SWEEPS + 1,)), dma((SWEEPS, CHIPS - 1)), dma((SWEEPS, CHIPS - 1)), dma, dma, dma,
    ]
    hbm = pl.BlockSpec(memory_space=pltpu.MemorySpace.HBM)
    anywhere = pl.BlockSpec(memory_space=pl.ANY)
    vmem = pl.BlockSpec(memory_space=pltpu.VMEM)
    return pl.pallas_call(
        body,
        out_shape=(
            jax.ShapeDtypeStruct((V, XS, 128), F32),
            jax.ShapeDtypeStruct((NM, XS, 128), F32),
        ),
        in_specs=[hbm] * 3 + [pl.BlockSpec(memory_space=pltpu.SMEM)] + [hbm] * 3,
        out_specs=(anywhere, vmem),
        scratch_shapes=scratch,
        name="solve",
        compiler_params=pltpu.CompilerParams(
            collective_id=0, has_side_effects=True, vmem_limit_bytes=48 * 2**20
        ),
    )(
        *(
            a if a is octant else pltpu.with_memory_space_constraint(a, pltpu.MemorySpace.HBM)
            for a in (distribution, speeds, weights.reshape(1, V), octant, inverses, inflow, solid_cells)
        )
    )


def solution(mesh):
    in_specs = (
        P("vel", "gx", None),
        P(None, "vel"),
        P("vel"),
        P("vel"),
        P(),
        P("vel", None),
        P("gx", None),
    )
    out_specs = (P("vel", "gx", None), P(None, "gx", None))
    return jax.shard_map(
        per_device, mesh=mesh, in_specs=in_specs, out_specs=out_specs, check_vma=False
    )
```

```python
import functools

import jax
import jax.numpy as jnp
from jax import lax
from jax.experimental import pallas as pl
from jax.experimental.pallas import tpu as pltpu
from jax.sharding import PartitionSpec as P


SHAKHOV = 4.0 / 45.0
KNUDSEN_STEP = 0.004
ABSORB = 0.3
SWEEPS = 2
MESH = pl.DeviceIdType.MESH
F32 = jnp.float32
BF16 = jnp.bfloat16

V = 432
H = 216
HP = 224
NC = 12
NM = 8
XS = 16
T = 32
PLANE = 32
ZX = 4
ZS = 8
CHIPS = 4
PARTS = 3


def split(x):
    hi = x.astype(BF16)
    return hi, (x - hi.astype(F32)).astype(BF16)


def dot(a, b):
    return jnp.dot(a, b, preferred_element_type=F32)


def rows_of(ax, ay, az, sx, sy, sz):
    cx, cy, cz = ax * sx, ay * sy, az * sz
    e = cx * cx + cy * cy + cz * cz
    f = e - 2.5
    one = jnp.ones_like(cx)
    phi = [one, cx, cy, cz, e * (2.0 / 3.0) - 1.0, cx * f, cy * f, cz * f]
    psi = [one, 2.0 * cx, 2.0 * cy, 2.0 * cz, e - 1.5, SHAKHOV * cx * f, SHAKHOV * cy * f, SHAKHOV * cz * f]
    return phi, psi


def body(
    dist, speeds_in, weights_in, octant, inverses, inflow, solid,
    out_h, out_m,
    speeds, weights, dx, spd, wall, wdir, inv, infl, sbuf, part0, part, own, rb1, rb2, mb, mo,
    b3, a3, at, abc, a32, ks, kc, kp, tsc, t2, gs, hloc, mloc, ebuf, esrc, hin, et, ec, kr, l3, wk, enat, abg,
    dsem, isem, ssend, srecv, rsend, rrecv, gsend, grecv, esend, erecv, osend, orecv, olocal,
):
    vel = lax.axis_index("vel")
    gx = lax.axis_index("gx")
    y = gx // 2
    c = gx % 2
    xi = vel // ZS
    zi = vel % ZS
    owner = (vel % 2) == c
    p = jnp.where(c == 0, y, CHIPS - 1 - y)

    def step_of(row, core):
        return jnp.where(core == 0, row, T - 1 - row)

    def classes_of(g):
        return [(8 * g + i) % NC for i in range(8)]

    def remote(src, dst, ss, rs, tv, tg):
        return pltpu.make_async_remote_copy(
            src_ref=src, dst_ref=dst, send_sem=ss, recv_sem=rs, device_id=(tv, tg), device_id_type=MESH
        )

    def send(src, dst, ss, rs, tv, tg, maybe=True):
        if not maybe:
            remote(src, dst, ss, rs, tv, tg).start()
            return
        here = (tv == vel) & (tg == gx)

        @pl.when(here)
        def _():
            pltpu.make_async_copy(src, dst, rs).start()

        @pl.when(jnp.logical_not(here))
        def _():
            remote(src, dst, ss, rs, tv, tg).start()

    small = [
        pltpu.make_async_copy(speeds_in, speeds, isem.at[2]),
        pltpu.make_async_copy(weights_in, weights, isem.at[3]),
    ]
    for copy in small:
        copy.start()
    for x in range(XS):
        pltpu.make_async_copy(dist.at[:, x, :], dx.at[x], dsem.at[x]).start()
    inv_copy = pltpu.make_async_copy(inverses, inv, isem.at[0])
    inv_copy.start()
    infl_copy = pltpu.make_async_copy(
        inflow.at[pl.ds(pl.multiple_of(c * H, 8), H)], infl.at[pl.ds(0, H)], isem.at[1]
    )
    infl_copy.start()

    barrier = pltpu.get_barrier_semaphore()

    def around(i):
        return lax.rem(zi + ZS // 2 + ((i + 1) // 2) * (2 * (i % 2) - 1) + ZS, ZS)

    def greet(i, _):
        tz = around(i)
        for o in (2, 1, 3, 0):
            tv = lax.rem(xi + o, ZX) * ZS + tz
            for cc in range(2):
                if o:
                    pl.semaphore_signal(barrier, inc=1, device_id=(tv, 2 * y + cc), device_id_type=MESH)
                    continue

                @pl.when(jnp.logical_not((tv == vel) & (cc == c)))
                def _():
                    pl.semaphore_signal(barrier, inc=1, device_id=(tv, 2 * y + cc), device_id_type=MESH)

        return 0

    lax.fori_loop(0, ZS, greet, 0)
    for o in range(1, CHIPS):
        for cc in range(2):
            pl.semaphore_signal(
                barrier, inc=1, device_id=(vel, lax.rem(y + o, CHIPS) * 2 + cc), device_id_type=MESH
            )

    lane = lax.broadcasted_iota(jnp.int32, (1, 512), 1)
    for copy in small:
        copy.wait()
    quadrant = octant[0]
    sy = (1 - 2 * lax.rem(quadrant, 2)).astype(F32)
    sz = (1 - 2 * lax.div(quadrant, 2)).astype(F32)
    spd[...] = jnp.zeros_like(spd)
    spd[0:3, 0:V] = speeds[...]
    spd[3:4, 0:V] = weights[...]
    sp = spd[...]
    sx_all = jnp.where(lane < H, 1.0, -1.0).astype(F32)
    phi, _ = rows_of(sp[0:1], sp[1:2], sp[2:3], sx_all, sy, sz)
    for m in range(NM):
        spd[m : m + 1, :] = phi[m] * sp[3:4]
    hi, lo = split(spd[...])
    wall[...] = jnp.concatenate([hi.astype(F32), lo.astype(F32)], axis=0).astype(BF16)

    for x in range(XS):
        pltpu.make_async_copy(dist.at[:, x, :], dx.at[x], dsem.at[x]).wait()
        hi, lo = split(dx[x])
        r = dot(wall[:, 0:V], jnp.concatenate([hi, lo], axis=1))
        part0[x] = r[0:8, 0:128] + r[8:16, 0:128] + r[0:8, 128:256] + r[8:16, 128:256]

    pl.semaphore_wait(barrier, 2 * PLANE - 1 + 2 * (CHIPS - 1))

    def rs1(i, _):
        tz = around(i)
        for o in range(2):
            row = (2 * c + o) * ZS + tz
            send(part0.at[o * ZS + tz], rb1.at[vel], rsend.at[0], rrecv.at[0], row, 2 * y + tz % 2)
        return 0

    lax.fori_loop(0, ZS, rs1, 0)

    for o in range(1, 2 * CHIPS):
        remote(solid, sbuf.at[gx], ssend, srecv, vel, lax.rem(gx + o, 2 * CHIPS)).start()
    pltpu.make_async_copy(solid, sbuf.at[gx], srecv).start()

    sp = jnp.where(c == 0, sp, pltpu.roll(sp, 512 - H, 1))
    sp = jnp.where(lane < H, sp, 0.0)
    sp = sp[:, 0:256]
    live = (lane < H).astype(F32)[:, 0:256]
    sx = (1 - 2 * c).astype(F32)
    phi, psi = rows_of(sp[0:1], sp[1:2], sp[2:3], sx, sy, sz)
    rate = sp[0:1] / (sp[0:1] + KNUDSEN_STEP)
    for m in range(NM):
        spd[m : m + 1, 0:256] = phi[m] * sp[3:4]
        spd[m : m + 1, 256:512] = psi[m] * ((1.0 - rate) * live)
    wd = spd[:, 0:256]
    ps = spd[:, 256:512]
    hi, lo = split(wd)
    wdir[...] = jnp.concatenate([hi.astype(F32), lo.astype(F32)], axis=0).astype(BF16)
    cls = lax.rem(lax.broadcasted_iota(jnp.int32, (8, 256), 1), NC)
    hi, lo = split(ps)
    hi, lo = hi.astype(F32), lo.astype(F32)
    abc[...] = jnp.broadcast_to(rate, (128, 256)).T[0:HP]
    for g in range(3):
        for i, k in enumerate(classes_of(g)):
            at[8 * i : 8 * i + 8] = jnp.where(cls == k, hi, 0.0)
            at[64 + 8 * i : 72 + 8 * i] = jnp.where(cls == k, lo, 0.0)
            at[128 + 8 * i : 136 + 8 * i] = jnp.where(cls == k, hi, 0.0)
        at[192:256] = jnp.zeros((64, 256), F32)
        table = at[...].T
        table = [table[8 * (3 * i + g) : 8 * (3 * i + g) + 8] for i in range(9)]
        table = jnp.concatenate(table + [jnp.zeros((8, 256), F32)], axis=0)
        a3[g] = table.astype(BF16)
        for i in range(9):
            abg[g, i] = abc[8 * (3 * i + g) : 8 * (3 * i + g) + 8]
    pw = abc[...]
    for _ in range(5):
        pw = pw * pw
    a32[...] = pw
    infl[H:HP] = jnp.zeros((HP - H, 128), F32)
    hloc[:, H:HP, :] = jnp.zeros((T, HP - H, 128), F32)
    infl_copy.wait()

    def powers(t, cur):
        cur = cur * rate
        tsc[t] = cur
        return cur

    lax.fori_loop(0, T, powers, wd)
    hi, lo = split(tsc[...].reshape(T * NM, 256))
    t2[0 : T * NM] = hi
    t2[T * NM : 2 * T * NM] = lo

    def remains(t, cur):
        tsc[T - 1 - t] = cur
        return cur * rate

    lax.fori_loop(0, T, remains, ps)
    late = tsc[...].reshape(T * NM, 256).T
    for d in range(2):
        et[d, 0:256] = late[:, 128 * d : 128 * d + 128]
        et[d, 256:288] = jnp.zeros((32, 128), F32)
    for k in range(NC):
        hi, lo = split(jnp.concatenate([et[d, pl.ds(k, 24, stride=NC), :] for d in range(2)], axis=1))
        ec[k] = jnp.concatenate([hi.astype(F32), lo.astype(F32)], axis=0).astype(BF16)

    def gather(rb, n, k, wait):
        @pl.when(owner)
        def _():
            full = rb.at[pl.ds(0, n)]
            remote(full, full, rsend.at[k], rrecv.at[k], vel, gx).wait_recv()
            own[k] = jnp.sum(rb[...].reshape(n // 8, 8, NM, 128), axis=0).sum(axis=0)

    gather(rb1, PLANE, 0, None)

    def spread(k, dst):
        @pl.when(owner)
        def _():
            def one(i, _):
                tz = around(i)
                for o in (2, 1, 3, 0):
                    tv = lax.rem(xi + o, ZX) * ZS + tz
                    for tc in range(2):
                        at_row = vel if tc == 0 else T - 1 - vel
                        send(own.at[k], dst.at[at_row], gsend.at[k], grecv.at[k], tv, 2 * y + tc, o == 0)
                return 0

            lax.fori_loop(0, ZS, one, 0)

    spread(0, mb.at[0])

    inv_copy.wait()
    ii = lax.broadcasted_iota(jnp.int32, (128, 128), 0)
    jj = lax.broadcasted_iota(jnp.int32, (128, 128), 1)
    perm = (ii == jnp.where(lax.rem(quadrant, 2) == 0, jj, 127 - jj)).astype(F32).astype(BF16)
    for n in range(NC // 2):
        parts = split(inv[2 * n : 2 * n + 2].reshape(256, 128))
        for q, w in enumerate(parts):
            u = lax.dot_general(perm, w, (((1,), (1,)), ((), ())), preferred_element_type=F32)
            u = jnp.concatenate([u[:, 0:128], u[:, 128:256]], axis=0).astype(BF16)
            v = dot(u, perm).astype(BF16)
            v = jnp.concatenate([v[0:128], v[128:256]], axis=1)
            cols = slice(256 * n, 256 * n + 256)
            if q == 0:
                b3[0:128, cols] = v
                b3[128:256, cols] = v
            else:
                b3[256:384, cols] = v

    remote(sbuf, sbuf, ssend, srecv, vel, gx).wait_recv()
    for chip in range(CHIPS):
        keep = 1.0 - ABSORB * sbuf[2 * chip : 2 * chip + 2].astype(F32).reshape(4, 8, 128)
        keep = (keep[0] * keep[1]) * (keep[2] * keep[3])
        for s in (4, 2, 1):
            keep = keep * pltpu.roll(keep, s, 0)
        kp[chip] = keep

    def cells(t, cur):
        x = step_of(t, c)
        keep = 1.0 - ABSORB * sbuf[2 * y + x // XS, pl.ds(x % XS, 1), :].astype(F32)
        keep = jnp.broadcast_to(keep, (8, 128))
        cur = cur * keep
        ks[t] = keep
        kc[t] = cur
        return cur

    lax.fori_loop(0, T, cells, jnp.ones((8, 128), F32))

    def left(t, cur):
        kr[T - 1 - t] = cur
        return cur * ks[T - 1 - t]

    lax.fori_loop(0, T, left, jnp.ones((8, 128), F32))

    for s in range(SWEEPS):
        remote(mb.at[s], mb.at[s], gsend.at[s], grecv.at[s], vel, gx).wait_recv()
        hi, lo = split(mb[s].reshape(T * NM, 128))
        l3[...] = jnp.concatenate([hi, lo, hi], axis=1)
        for part_of in range(PARTS):
            for n in range(2 * part_of, 2 * part_of + 2):
                g = dot(l3[...], b3[:, 256 * n : 256 * n + 256]).reshape(T, NM, 256)
                gs[:, 16 * n : 16 * n + 16, :] = jnp.concatenate([g[:, :, 0:128], g[:, :, 128:256]], axis=1)
                for d in range(2):
                    hi, lo = split((g[:, :, 128 * d : 128 * d + 128] * kr[...]).reshape(T * NM, 128))
                    wk[2 * n + d] = jnp.concatenate([hi, lo], axis=1)
            for d in range(4):
                r = dot(ec[4 * part_of + d], wk[4 * part_of + d])
                r = r[0:24, 0:128] + r[24:48, 0:128] + r[0:24, 128:256]
                esrc[s, part_of, pl.ds(d, H // NC, stride=4), :] = r[0 : H // NC]

            for gap in (2, 1, 3):
                q = p + gap

                @pl.when(q < CHIPS)
                def _():
                    ty = jnp.where(c == 0, q, CHIPS - 1 - q)
                    remote(
                        esrc.at[s, part_of], ebuf.at[s, p, part_of], esend.at[s, gap - 1], erecv.at[s, p],
                        vel, 2 * ty + c,
                    ).start()

        def march(u, h):
            t = 2 * u
            hi, lo = split(jnp.concatenate([gs[t], gs[t + 1]], axis=1))
            after = []
            for g in range(3):
                pairs = [k // 2 for k in classes_of(g)[::2]]
                hs = [hi[16 * n : 16 * n + 16] for n in pairs]
                ls = [lo[16 * n : 16 * n + 16] for n in pairs]
                r = dot(a3[g, :, 0:192], jnp.concatenate(hs + hs + ls, axis=0))
                now = h[g]
                for d in range(2):
                    now = now * (abg[g] * ks[t + d][None]) + r[0:72, 128 * d : 128 * d + 128].reshape(9, 8, 128)
                    for i in range(9):
                        hloc[t + d, 8 * (3 * i + g) : 8 * (3 * i + g) + 8, :] = now[i]
                after.append(now)
            return tuple(after)

        lax.fori_loop(0, T // 2, march, (jnp.zeros((9, 8, 128), F32),) * 3, unroll=2)

        def local_moments(u, _):
            t = 2 * u
            hi, lo = split(jnp.concatenate([hloc[t], hloc[t + 1]], axis=1))
            r = dot(wdir[:, 0:HP], hi) + dot(wdir[:, 0:HP], lo)
            r = r[0:8] + r[8:16]
            mloc[t] = r[:, 0:128]
            mloc[t + 1] = r[:, 128:256]
            return 0

        lax.fori_loop(0, T // 2, local_moments, 0, unroll=2)

        hin[...] = infl[...]
        for q in range(CHIPS - 1):

            @pl.when(q < p)
            def _():
                full = ebuf.at[s, q]
                remote(full, full, esend.at[s, 0], erecv.at[s, q], vel, gx).wait_recv()
                k = kp[jnp.where(c == 0, q, CHIPS - 1 - q)]
                span = a32[...].reshape(HP // 8, 8, 128) * k[None]
                now = hin[...].reshape(HP // 8, 8, 128) * span
                for k in range(NC):
                    own_rows = pl.ds(k, H // NC, stride=NC)
                    enat[own_rows, :] = ebuf[s, q, k // 4, pl.ds(k % 4, H // NC, stride=4), :]
                now = now[0 : H // 8] + enat[...].reshape(H // 8, 8, 128)
                hin[0:H] = now.reshape(H, 128)

        hi, lo = split(hin[...])
        r = dot(t2[:, 0:HP], jnp.concatenate([hi, lo], axis=1))
        n = T * NM
        r = (r[0:n, 0:128] + r[n : 2 * n, 0:128]) + (r[0:n, 128:256] + r[n : 2 * n, 128:256])
        part[s] = mloc[...] + kc[...] * r.reshape(T, NM, 128)

        def rs(i, _):
            tz = around(i)
            for o in (2, 1, 3, 0):
                row = lax.rem(xi + o, ZX) * ZS + tz
                send(
                    part.at[s, step_of(row, c)], rb2.at[s, 2 * vel + c], rsend.at[s + 1], rrecv.at[s + 1],
                    row, 2 * y + tz % 2, o == 0,
                )
            return 0

        lax.fori_loop(0, ZS, rs, 0)

        if s == SWEEPS - 1:
            def finish(t, h):
                a = abc[...].reshape(HP // 8, 8, 128)
                h = h * (a * ks[t][None])
                hloc[t] = (hloc[t].reshape(HP // 8, 8, 128) + h).reshape(HP, 128)
                return h

            first = pl.multiple_of(c * H, 8)

            def far(t, h):
                h = finish(t, h)
                x = jnp.where(c == 0, t - XS, T - 1 - t)
                remote(
                    hloc.at[t, pl.ds(0, H)], out_h.at[pl.ds(first, H), x, :], osend, orecv, vel, 2 * y + 1 - c
                ).start()
                return h

            def near(t, h):
                h = finish(t, h)
                x = jnp.where(c == 0, t, XS - 1 - t)
                pltpu.make_async_copy(hloc.at[t, pl.ds(0, H)], out_h.at[pl.ds(first, H), x, :], olocal).start()
                return h

            h = lax.fori_loop(0, XS, near, hin[...].reshape(HP // 8, 8, 128))
            lax.fori_loop(XS, T, far, h)

        gather(rb2.at[s], 2 * PLANE, s + 1, None)
        if s < SWEEPS - 1:
            spread(s + 1, mb.at[s + 1])

    last = SWEEPS
    section = vel // XS

    @pl.when(owner)
    def _():
        def one(i, _):
            tz = around(i)
            for o in (2, 1, 3, 0):
                tv = lax.rem(xi + o, ZX) * ZS + tz
                send(own.at[last], mo.at[vel % XS], gsend.at[last], grecv.at[last], tv, 2 * y + section, o == 0)
            return 0

        lax.fori_loop(0, ZS, one, 0)

    remote(mo, mo, gsend.at[last], grecv.at[last], vel, gx).wait_recv()
    for x in range(XS):
        out_m[:, x, :] = mo[x]

    for o in range(1, 2 * CHIPS):
        remote(solid, sbuf.at[gx], ssend, srecv, vel, gx).wait_send()
    mine = owner & (section == c)

    def drain(buf, n, less, sem):
        @pl.when(less)
        def _():
            remote(buf.at[pl.ds(0, n - 1)], buf.at[pl.ds(0, n - 1)], sem, sem, vel, gx).wait_send()

        @pl.when(jnp.logical_not(less))
        def _():
            remote(buf.at[pl.ds(0, n)], buf.at[pl.ds(0, n)], sem, sem, vel, gx).wait_send()

    drain(part0, XS, mine, rsend.at[0])
    for s in range(SWEEPS):
        drain(part.at[s], T, owner, rsend.at[s + 1])
        for gap in (2, 1, 3):

            @pl.when(p + gap < CHIPS)
            def _():
                remote(esrc.at[s], esrc.at[s], esend.at[s, gap - 1], esend.at[s, gap - 1], vel, gx).wait_send()

    @pl.when(owner)
    def _():
        for k in range(SWEEPS):
            few = rb2.at[0, pl.ds(0, 2 * PLANE - 1)]
            remote(few, few, gsend.at[k], gsend.at[k], vel, gx).wait_send()
        drain(rb2.at[0], PLANE, section == c, gsend.at[last])

    half = hloc.at[pl.ds(0, XS), pl.ds(0, H)]
    remote(half, half, osend, orecv, vel, gx).wait()
    pltpu.make_async_copy(half, half, olocal).wait()


def per_device(distribution, speeds, weights, octant, inverses, inflow, solid_cells):
    dma = pltpu.SemaphoreType.DMA
    vm = pltpu.VMEM
    scratch = [
        vm((3, V), F32), vm((1, V), F32),
        vm((XS, V, 128), F32), vm((8, 512), F32), vm((16, 512), BF16), vm((16, 256), BF16),
        vm((NC, 128, 128), F32), vm((HP, 128), F32), vm((2 * CHIPS, XS, 128), jnp.int32),
        vm((XS, NM, 128), F32), vm((SWEEPS, T, NM, 128), F32), vm((SWEEPS + 1, NM, 128), F32),
        vm((PLANE, NM, 128), F32), vm((SWEEPS, 2 * PLANE, NM, 128), F32), vm((SWEEPS, T, NM, 128), F32),
        vm((XS, NM, 128), F32),
        vm((384, NC * 128), BF16), vm((3, 80, 256), BF16), vm((256, 256), F32), vm((HP, 128), F32),
        vm((HP, 128), F32), vm((T, 8, 128), F32), vm((T, 8, 128), F32), vm((CHIPS, 8, 128), F32),
        vm((T, 8, 256), F32), vm((2 * T * NM, 256), BF16), vm((T, 96, 128), F32), vm((T, HP, 128), F32),
        vm((T, NM, 128), F32), vm((SWEEPS, CHIPS - 1, PARTS, H // PARTS, 128), F32),
        vm((SWEEPS, PARTS, H // PARTS, 128), F32),
        vm((HP, 128), F32), vm((2, 288, 128), F32), vm((NC, 48, 256), BF16), vm((T, 8, 128), F32),
        vm((T * NM, 384), BF16), vm((NC, T * NM, 256), BF16), vm((H, 128), F32), vm((3, 9, 8, 128), F32),
        dma((XS,)), dma((4,)), dma, dma, dma((SWEEPS + 1,)), dma((SWEEPS + 1,)), dma((SWEEPS + 1,)),
        dma((SWEEPS + 1,)), dma((SWEEPS, CHIPS - 1)), dma((SWEEPS, CHIPS - 1)), dma, dma, dma,
    ]
    hbm = pl.BlockSpec(memory_space=pltpu.MemorySpace.HBM)
    anywhere = pl.BlockSpec(memory_space=pl.ANY)
    vmem = pl.BlockSpec(memory_space=pltpu.VMEM)
    field, fields = pl.pallas_call(
        body,
        out_shape=(
            jax.ShapeDtypeStruct((V, XS, 128), F32),
            jax.ShapeDtypeStruct((NM, XS, 128), F32),
        ),
        in_specs=[hbm] * 3 + [pl.BlockSpec(memory_space=pltpu.SMEM)] + [hbm] * 3,
        out_specs=(anywhere, vmem),
        scratch_shapes=scratch,
        name="solve",
        compiler_params=pltpu.CompilerParams(
            collective_id=0, has_side_effects=True, vmem_limit_bytes=48 * 2**20
        ),
    )(
        *(
            a if a is octant else pltpu.with_memory_space_constraint(a, pltpu.MemorySpace.HBM)
            for a in (distribution, speeds, weights.reshape(1, V), octant, inverses, inflow, solid_cells)
        )
    )
    parts = 4

    def store(a, b, out_a, out_b, sems):
        copies = [pltpu.make_async_copy(b, out_b, sems.at[parts])]
        for i in range(parts):
            some = pl.ds(i * (V // parts), V // parts)
            copies.append(pltpu.make_async_copy(a.at[some], out_a.at[some], sems.at[i]))
        for copy in copies:
            copy.start()
        for copy in copies:
            copy.wait()

    return pl.pallas_call(
        store,
        out_shape=(
            jax.ShapeDtypeStruct(field.shape, F32),
            jax.ShapeDtypeStruct(fields.shape, F32),
        ),
        in_specs=[anywhere, anywhere],
        out_specs=(hbm, hbm),
        scratch_shapes=[dma((parts + 1,))],
        name="store",
        compiler_params=pltpu.CompilerParams(vmem_limit_bytes=2**20),
    )(field, fields)


def solution(mesh):
    in_specs = (
        P("vel", "gx", None),
        P(None, "vel"),
        P("vel"),
        P("vel"),
        P(),
        P("vel", None),
        P("gx", None),
    )
    out_specs = (P("vel", "gx", None), P(None, "gx", None))
    return jax.shard_map(
        per_device, mesh=mesh, in_specs=in_specs, out_specs=out_specs, check_vma=False
    )
```

```python
import functools

import jax
import jax.numpy as jnp
from jax import lax
from jax.experimental import pallas as pl
from jax.experimental.pallas import tpu as pltpu
from jax.sharding import PartitionSpec as P


SHAKHOV = 4.0 / 45.0
KNUDSEN_STEP = 0.004
ABSORB = 0.3
SWEEPS = 2
MESH = pl.DeviceIdType.MESH
F32 = jnp.float32
BF16 = jnp.bfloat16

V = 432
H = 216
HP = 224
NC = 12
NM = 8
XS = 16
T = 32
PLANE = 32
ZX = 4
ZS = 8
CHIPS = 4
PARTS = 3


def split(x):
    hi = x.astype(BF16)
    return hi, (x - hi.astype(F32)).astype(BF16)


def dot(a, b):
    return jnp.dot(a, b, preferred_element_type=F32)


def rows_of(ax, ay, az, sx, sy, sz):
    cx, cy, cz = ax * sx, ay * sy, az * sz
    e = cx * cx + cy * cy + cz * cz
    f = e - 2.5
    one = jnp.ones_like(cx)
    phi = [one, cx, cy, cz, e * (2.0 / 3.0) - 1.0, cx * f, cy * f, cz * f]
    psi = [one, 2.0 * cx, 2.0 * cy, 2.0 * cz, e - 1.5, SHAKHOV * cx * f, SHAKHOV * cy * f, SHAKHOV * cz * f]
    return phi, psi


def body(
    dist, speeds_in, weights_in, octant, inverses, inflow, solid,
    out_h, out_m,
    speeds, weights, dx, spd, wall, wdir, inv, infl, sbuf, part0, part, own, rb1, first, rb2, mb, mo,
    b3, a3, at, abc, a32, ks, kc, kp, tsc, t2, gs, hloc, mloc, ebuf, esrc, hin, et, ec, kr, l3, wk, enat, abg,
    dsem, isem, ssend, srecv, rsend, rrecv, gsend, grecv, esend, erecv, osend, orecv, olocal,
):
    vel = lax.axis_index("vel")
    gx = lax.axis_index("gx")
    y = gx // 2
    c = gx % 2
    xi = vel // ZS
    zi = vel % ZS
    owner = (vel % 2) == c
    p = jnp.where(c == 0, y, CHIPS - 1 - y)

    def step_of(row, core):
        return jnp.where(core == 0, row, T - 1 - row)

    def classes_of(g):
        return [(8 * g + i) % NC for i in range(8)]

    def remote(src, dst, ss, rs, tv, tg):
        return pltpu.make_async_remote_copy(
            src_ref=src, dst_ref=dst, send_sem=ss, recv_sem=rs, device_id=(tv, tg), device_id_type=MESH
        )

    def send(src, dst, ss, rs, tv, tg, maybe=True):
        if not maybe:
            remote(src, dst, ss, rs, tv, tg).start()
            return
        here = (tv == vel) & (tg == gx)

        @pl.when(here)
        def _():
            pltpu.make_async_copy(src, dst, rs).start()

        @pl.when(jnp.logical_not(here))
        def _():
            remote(src, dst, ss, rs, tv, tg).start()

    small = [
        pltpu.make_async_copy(speeds_in, speeds, isem.at[2]),
        pltpu.make_async_copy(weights_in, weights, isem.at[3]),
    ]
    for copy in small:
        copy.start()
    for x in range(XS):
        pltpu.make_async_copy(dist.at[:, x, :], dx.at[x], dsem.at[x]).start()
    inv_copy = pltpu.make_async_copy(inverses, inv, isem.at[0])
    inv_copy.start()
    infl_copy = pltpu.make_async_copy(
        inflow.at[pl.ds(pl.multiple_of(c * H, 8), H)], infl.at[pl.ds(0, H)], isem.at[1]
    )
    infl_copy.start()

    barrier = pltpu.get_barrier_semaphore()

    def around(i):
        return lax.rem(zi + ZS // 2 + ((i + 1) // 2) * (2 * (i % 2) - 1) + ZS, ZS)

    def greet(i, _):
        tz = around(i)
        for o in (2, 1, 3, 0):
            tv = lax.rem(xi + o, ZX) * ZS + tz
            for cc in range(2):
                if o:
                    pl.semaphore_signal(barrier, inc=1, device_id=(tv, 2 * y + cc), device_id_type=MESH)
                    continue

                @pl.when(jnp.logical_not((tv == vel) & (cc == c)))
                def _():
                    pl.semaphore_signal(barrier, inc=1, device_id=(tv, 2 * y + cc), device_id_type=MESH)

        return 0

    lax.fori_loop(0, ZS, greet, 0)
    for o in range(1, CHIPS):
        for cc in range(2):
            pl.semaphore_signal(
                barrier, inc=1, device_id=(vel, lax.rem(y + o, CHIPS) * 2 + cc), device_id_type=MESH
            )

    lane = lax.broadcasted_iota(jnp.int32, (1, 512), 1)
    for copy in small:
        copy.wait()
    quadrant = octant[0]
    sy = (1 - 2 * lax.rem(quadrant, 2)).astype(F32)
    sz = (1 - 2 * lax.div(quadrant, 2)).astype(F32)
    spd[...] = jnp.zeros_like(spd)
    spd[0:3, 0:V] = speeds[...]
    spd[3:4, 0:V] = weights[...]
    sp = spd[...]
    sx_all = jnp.where(lane < H, 1.0, -1.0).astype(F32)
    phi, _ = rows_of(sp[0:1], sp[1:2], sp[2:3], sx_all, sy, sz)
    for m in range(NM):
        spd[m : m + 1, :] = phi[m] * sp[3:4]
    hi, lo = split(spd[...])
    wall[...] = jnp.concatenate([hi.astype(F32), lo.astype(F32)], axis=0).astype(BF16)

    for x in range(XS):
        pltpu.make_async_copy(dist.at[:, x, :], dx.at[x], dsem.at[x]).wait()
        hi, lo = split(dx[x])
        r = dot(wall[:, 0:V], jnp.concatenate([hi, lo], axis=1))
        part0[x] = r[0:8, 0:128] + r[8:16, 0:128] + r[0:8, 128:256] + r[8:16, 128:256]

    pl.semaphore_wait(barrier, 2 * PLANE - 1 + 2 * (CHIPS - 1))

    def rs1(i, _):
        tz = around(i)
        for o in range(2):
            tv = (2 * c + o) * ZS + tz
            for far in range(2):
                row = o * ZS + lax.rem(tz + far * (ZS // 2), ZS)
                send(part0.at[row], rb1.at[far, vel], rsend.at[0], rrecv.at[0], tv, 2 * y + tz % 2)
        return 0

    lax.fori_loop(0, ZS, rs1, 0)

    for o in range(1, 2 * CHIPS):
        remote(solid, sbuf.at[gx], ssend, srecv, vel, lax.rem(gx + o, 2 * CHIPS)).start()
    pltpu.make_async_copy(solid, sbuf.at[gx], srecv).start()

    sp = jnp.where(c == 0, sp, pltpu.roll(sp, 512 - H, 1))
    sp = jnp.where(lane < H, sp, 0.0)
    sp = sp[:, 0:256]
    live = (lane < H).astype(F32)[:, 0:256]
    sx = (1 - 2 * c).astype(F32)
    phi, psi = rows_of(sp[0:1], sp[1:2], sp[2:3], sx, sy, sz)
    rate = sp[0:1] / (sp[0:1] + KNUDSEN_STEP)
    for m in range(NM):
        spd[m : m + 1, 0:256] = phi[m] * sp[3:4]
        spd[m : m + 1, 256:512] = psi[m] * ((1.0 - rate) * live)
    wd = spd[:, 0:256]
    ps = spd[:, 256:512]
    hi, lo = split(wd)
    wdir[...] = jnp.concatenate([hi.astype(F32), lo.astype(F32)], axis=0).astype(BF16)
    cls = lax.rem(lax.broadcasted_iota(jnp.int32, (8, 256), 1), NC)
    hi, lo = split(ps)
    hi, lo = hi.astype(F32), lo.astype(F32)
    abc[...] = jnp.broadcast_to(rate, (128, 256)).T[0:HP]
    for g in range(3):
        for i, k in enumerate(classes_of(g)):
            at[8 * i : 8 * i + 8] = jnp.where(cls == k, hi, 0.0)
            at[64 + 8 * i : 72 + 8 * i] = jnp.where(cls == k, lo, 0.0)
            at[128 + 8 * i : 136 + 8 * i] = jnp.where(cls == k, hi, 0.0)
        at[192:256] = jnp.zeros((64, 256), F32)
        table = at[...].T
        table = [table[8 * (3 * i + g) : 8 * (3 * i + g) + 8] for i in range(9)]
        table = jnp.concatenate(table + [jnp.zeros((8, 256), F32)], axis=0)
        a3[g] = table.astype(BF16)
        for i in range(9):
            abg[g, i] = abc[8 * (3 * i + g) : 8 * (3 * i + g) + 8]
    pw = abc[...]
    for _ in range(5):
        pw = pw * pw
    a32[...] = pw
    infl[H:HP] = jnp.zeros((HP - H, 128), F32)
    hloc[:, H:HP, :] = jnp.zeros((T, HP - H, 128), F32)
    infl_copy.wait()

    def powers(t, cur):
        cur = cur * rate
        tsc[t] = cur
        return cur

    lax.fori_loop(0, T, powers, wd)
    hi, lo = split(tsc[...].reshape(T * NM, 256))
    t2[0 : T * NM] = hi
    t2[T * NM : 2 * T * NM] = lo

    def remains(t, cur):
        tsc[T - 1 - t] = cur
        return cur * rate

    lax.fori_loop(0, T, remains, ps)
    late = tsc[...].reshape(T * NM, 256).T
    for d in range(2):
        et[d, 0:256] = late[:, 128 * d : 128 * d + 128]
        et[d, 256:288] = jnp.zeros((32, 128), F32)
    for k in range(NC):
        hi, lo = split(jnp.concatenate([et[d, pl.ds(k, 24, stride=NC), :] for d in range(2)], axis=1))
        ec[k] = jnp.concatenate([hi.astype(F32), lo.astype(F32)], axis=0).astype(BF16)

    def gather(rb, n, k, wait):
        @pl.when(owner)
        def _():
            full = rb.at[pl.ds(0, n)]
            remote(full, full, rsend.at[k], rrecv.at[k], vel, gx).wait_recv()
            own[k - 1] = jnp.sum(rb[...].reshape(n // 8, 8, NM, 128), axis=0).sum(axis=0)

    @pl.when(owner)
    def _():
        remote(rb1, rb1, rsend.at[0], rrecv.at[0], vel, gx).wait_recv()
        for far in range(2):
            first[far] = jnp.sum(rb1[far].reshape(PLANE // 8, 8, NM, 128), axis=0).sum(axis=0)

        def one(i, _):
            tz = lax.rem(zi + ZS + (1 - i % 2) * (i // 2 - 2) + (i % 2) * (1 - i // 2), ZS)
            for o in (2, 1, 3, 0):
                tv = lax.rem(xi + o, ZX) * ZS + tz
                for tc in range(2):
                    for far in range(2):
                        row = xi * ZS + lax.rem(zi + far * (ZS // 2), ZS)
                        at_row = row if tc == 0 else T - 1 - row
                        send(first.at[far], mb.at[0, at_row], gsend.at[0], grecv.at[0], tv, 2 * y + tc, o == 0)
            return 0

        lax.fori_loop(0, 4, one, 0)

    def spread(k, dst):
        @pl.when(owner)
        def _():
            def one(i, _):
                tz = around(i)
                for o in (2, 1, 3, 0):
                    tv = lax.rem(xi + o, ZX) * ZS + tz
                    for tc in range(2):
                        at_row = vel if tc == 0 else T - 1 - vel
                        send(own.at[k - 1], dst.at[at_row], gsend.at[k], grecv.at[k], tv, 2 * y + tc, o == 0)
                return 0

            lax.fori_loop(0, ZS, one, 0)


    inv_copy.wait()
    ii = lax.broadcasted_iota(jnp.int32, (128, 128), 0)
    jj = lax.broadcasted_iota(jnp.int32, (128, 128), 1)
    perm = (ii == jnp.where(lax.rem(quadrant, 2) == 0, jj, 127 - jj)).astype(F32).astype(BF16)
    for n in range(NC // 2):
        parts = split(inv[2 * n : 2 * n + 2].reshape(256, 128))
        for q, w in enumerate(parts):
            u = lax.dot_general(perm, w, (((1,), (1,)), ((), ())), preferred_element_type=F32)
            u = jnp.concatenate([u[:, 0:128], u[:, 128:256]], axis=0).astype(BF16)
            v = dot(u, perm).astype(BF16)
            v = jnp.concatenate([v[0:128], v[128:256]], axis=1)
            cols = slice(256 * n, 256 * n + 256)
            if q == 0:
                b3[0:128, cols] = v
                b3[128:256, cols] = v
            else:
                b3[256:384, cols] = v

    remote(sbuf, sbuf, ssend, srecv, vel, gx).wait_recv()
    for chip in range(CHIPS):
        keep = 1.0 - ABSORB * sbuf[2 * chip : 2 * chip + 2].astype(F32).reshape(4, 8, 128)
        keep = (keep[0] * keep[1]) * (keep[2] * keep[3])
        for s in (4, 2, 1):
            keep = keep * pltpu.roll(keep, s, 0)
        kp[chip] = keep

    def cells(t, cur):
        x = step_of(t, c)
        keep = 1.0 - ABSORB * sbuf[2 * y + x // XS, pl.ds(x % XS, 1), :].astype(F32)
        keep = jnp.broadcast_to(keep, (8, 128))
        cur = cur * keep
        ks[t] = keep
        kc[t] = cur
        return cur

    lax.fori_loop(0, T, cells, jnp.ones((8, 128), F32))

    def left(t, cur):
        kr[T - 1 - t] = cur
        return cur * ks[T - 1 - t]

    lax.fori_loop(0, T, left, jnp.ones((8, 128), F32))

    for s in range(SWEEPS):
        remote(mb.at[s], mb.at[s], gsend.at[s], grecv.at[s], vel, gx).wait_recv()
        hi, lo = split(mb[s].reshape(T * NM, 128))
        l3[...] = jnp.concatenate([hi, lo, hi], axis=1)
        for part_of in range(PARTS):
            for n in range(2 * part_of, 2 * part_of + 2):
                g = dot(l3[...], b3[:, 256 * n : 256 * n + 256]).reshape(T, NM, 256)
                gs[:, 16 * n : 16 * n + 16, :] = jnp.concatenate([g[:, :, 0:128], g[:, :, 128:256]], axis=1)
                for d in range(2):
                    hi, lo = split((g[:, :, 128 * d : 128 * d + 128] * kr[...]).reshape(T * NM, 128))
                    wk[2 * n + d] = jnp.concatenate([hi, lo], axis=1)
            for d in range(4):
                r = dot(ec[4 * part_of + d], wk[4 * part_of + d])
                r = r[0:24, 0:128] + r[24:48, 0:128] + r[0:24, 128:256]
                esrc[s, part_of, pl.ds(d, H // NC, stride=4), :] = r[0 : H // NC]

            for gap in (2, 1, 3):
                q = p + gap

                @pl.when(q < CHIPS)
                def _():
                    ty = jnp.where(c == 0, q, CHIPS - 1 - q)
                    remote(
                        esrc.at[s, part_of], ebuf.at[s, p, part_of], esend.at[s, gap - 1], erecv.at[s, p],
                        vel, 2 * ty + c,
                    ).start()

        def march(u, h):
            t = 2 * u
            hi, lo = split(jnp.concatenate([gs[t], gs[t + 1]], axis=1))
            after = []
            for g in range(3):
                pairs = [k // 2 for k in classes_of(g)[::2]]
                hs = [hi[16 * n : 16 * n + 16] for n in pairs]
                ls = [lo[16 * n : 16 * n + 16] for n in pairs]
                r = dot(a3[g, :, 0:192], jnp.concatenate(hs + hs + ls, axis=0))
                now = h[g]
                for d in range(2):
                    now = now * (abg[g] * ks[t + d][None]) + r[0:72, 128 * d : 128 * d + 128].reshape(9, 8, 128)
                    for i in range(9):
                        hloc[t + d, 8 * (3 * i + g) : 8 * (3 * i + g) + 8, :] = now[i]
                after.append(now)
            return tuple(after)

        lax.fori_loop(0, T // 2, march, (jnp.zeros((9, 8, 128), F32),) * 3, unroll=4)

        def local_moments(u, _):
            t = 2 * u
            hi, lo = split(jnp.concatenate([hloc[t], hloc[t + 1]], axis=1))
            r = dot(wdir[:, 0:HP], hi) + dot(wdir[:, 0:HP], lo)
            r = r[0:8] + r[8:16]
            mloc[t] = r[:, 0:128]
            mloc[t + 1] = r[:, 128:256]
            return 0

        lax.fori_loop(0, T // 2, local_moments, 0, unroll=4)

        hin[...] = infl[...]
        for q in range(CHIPS - 1):

            @pl.when(q < p)
            def _():
                full = ebuf.at[s, q]
                remote(full, full, esend.at[s, 0], erecv.at[s, q], vel, gx).wait_recv()
                k = kp[jnp.where(c == 0, q, CHIPS - 1 - q)]
                span = a32[...].reshape(HP // 8, 8, 128) * k[None]
                now = hin[...].reshape(HP // 8, 8, 128) * span
                for k in range(NC):
                    own_rows = pl.ds(k, H // NC, stride=NC)
                    enat[own_rows, :] = ebuf[s, q, k // 4, pl.ds(k % 4, H // NC, stride=4), :]
                now = now[0 : H // 8] + enat[...].reshape(H // 8, 8, 128)
                hin[0:H] = now.reshape(H, 128)

        hi, lo = split(hin[...])
        r = dot(t2[:, 0:HP], jnp.concatenate([hi, lo], axis=1))
        n = T * NM
        r = (r[0:n, 0:128] + r[n : 2 * n, 0:128]) + (r[0:n, 128:256] + r[n : 2 * n, 128:256])
        part[s] = mloc[...] + kc[...] * r.reshape(T, NM, 128)

        def rs(i, _):
            tz = around(i)
            for o in (2, 1, 3, 0):
                row = lax.rem(xi + o, ZX) * ZS + tz
                send(
                    part.at[s, step_of(row, c)], rb2.at[s, 2 * vel + c], rsend.at[s + 1], rrecv.at[s + 1],
                    row, 2 * y + tz % 2, o == 0,
                )
            return 0

        lax.fori_loop(0, ZS, rs, 0)

        if s == SWEEPS - 1:
            def finish(t, h):
                a = abc[...].reshape(HP // 8, 8, 128)
                h = h * (a * ks[t][None])
                hloc[t] = (hloc[t].reshape(HP // 8, 8, 128) + h).reshape(HP, 128)
                return h

            start = pl.multiple_of(c * H, 8)

            def far(t, h):
                h = finish(t, h)
                x = jnp.where(c == 0, t - XS, T - 1 - t)
                remote(
                    hloc.at[t, pl.ds(0, H)], out_h.at[pl.ds(start, H), x, :], osend, orecv, vel, 2 * y + 1 - c
                ).start()
                return h

            def near(t, h):
                h = finish(t, h)
                x = jnp.where(c == 0, t, XS - 1 - t)
                pltpu.make_async_copy(hloc.at[t, pl.ds(0, H)], out_h.at[pl.ds(start, H), x, :], olocal).start()
                return h

            h = lax.fori_loop(0, XS, near, hin[...].reshape(HP // 8, 8, 128))
            lax.fori_loop(XS, T, far, h)

        gather(rb2.at[s], 2 * PLANE, s + 1, None)
        if s < SWEEPS - 1:
            spread(s + 1, mb.at[s + 1])

    last = SWEEPS
    section = vel // XS

    @pl.when(owner)
    def _():
        def one(i, _):
            tz = around(i)
            for o in (2, 1, 3, 0):
                tv = lax.rem(xi + o, ZX) * ZS + tz
                send(own.at[last - 1], mo.at[vel % XS], gsend.at[last], grecv.at[last], tv, 2 * y + section, o == 0)
            return 0

        lax.fori_loop(0, ZS, one, 0)

    remote(mo, mo, gsend.at[last], grecv.at[last], vel, gx).wait_recv()
    for x in range(XS):
        out_m[:, x, :] = mo[x]

    for o in range(1, 2 * CHIPS):
        remote(solid, sbuf.at[gx], ssend, srecv, vel, gx).wait_send()
    mine = owner & (section == c)

    def drain(buf, n, less, sem, by=1):
        @pl.when(less)
        def _():
            remote(buf.at[pl.ds(0, n - by)], buf.at[pl.ds(0, n - by)], sem, sem, vel, gx).wait_send()

        @pl.when(jnp.logical_not(less))
        def _():
            remote(buf.at[pl.ds(0, n)], buf.at[pl.ds(0, n)], sem, sem, vel, gx).wait_send()

    drain(rb1.at[0], 2 * XS, mine, rsend.at[0], 2)
    for s in range(SWEEPS):
        drain(part.at[s], T, owner, rsend.at[s + 1])
        for gap in (2, 1, 3):

            @pl.when(p + gap < CHIPS)
            def _():
                remote(esrc.at[s], esrc.at[s], esend.at[s, gap - 1], esend.at[s, gap - 1], vel, gx).wait_send()

    @pl.when(owner)
    def _():
        for k in range(SWEEPS):
            few = rb2.at[0, pl.ds(0, 2 * PLANE - (2 if k == 0 else 1))]
            remote(few, few, gsend.at[k], gsend.at[k], vel, gx).wait_send()
        drain(rb2.at[0], PLANE, section == c, gsend.at[last])

    half = hloc.at[pl.ds(0, XS), pl.ds(0, H)]
    remote(half, half, osend, orecv, vel, gx).wait()
    pltpu.make_async_copy(half, half, olocal).wait()


def per_device(distribution, speeds, weights, octant, inverses, inflow, solid_cells):
    dma = pltpu.SemaphoreType.DMA
    vm = pltpu.VMEM
    scratch = [
        vm((3, V), F32), vm((1, V), F32),
        vm((XS, V, 128), F32), vm((8, 512), F32), vm((16, 512), BF16), vm((16, 256), BF16),
        vm((NC, 128, 128), F32), vm((HP, 128), F32), vm((2 * CHIPS, XS, 128), jnp.int32),
        vm((XS, NM, 128), F32), vm((SWEEPS, T, NM, 128), F32), vm((SWEEPS, NM, 128), F32),
        vm((2, PLANE, NM, 128), F32), vm((2, NM, 128), F32), vm((SWEEPS, 2 * PLANE, NM, 128), F32), vm((SWEEPS, T, NM, 128), F32),
        vm((XS, NM, 128), F32),
        vm((384, NC * 128), BF16), vm((3, 80, 256), BF16), vm((256, 256), F32), vm((HP, 128), F32),
        vm((HP, 128), F32), vm((T, 8, 128), F32), vm((T, 8, 128), F32), vm((CHIPS, 8, 128), F32),
        vm((T, 8, 256), F32), vm((2 * T * NM, 256), BF16), vm((T, 96, 128), F32), vm((T, HP, 128), F32),
        vm((T, NM, 128), F32), vm((SWEEPS, CHIPS - 1, PARTS, H // PARTS, 128), F32),
        vm((SWEEPS, PARTS, H // PARTS, 128), F32),
        vm((HP, 128), F32), vm((2, 288, 128), F32), vm((NC, 48, 256), BF16), vm((T, 8, 128), F32),
        vm((T * NM, 384), BF16), vm((NC, T * NM, 256), BF16), vm((H, 128), F32), vm((3, 9, 8, 128), F32),
        dma((XS,)), dma((4,)), dma, dma, dma((SWEEPS + 1,)), dma((SWEEPS + 1,)), dma((SWEEPS + 1,)),
        dma((SWEEPS + 1,)), dma((SWEEPS, CHIPS - 1)), dma((SWEEPS, CHIPS - 1)), dma, dma, dma,
    ]
    hbm = pl.BlockSpec(memory_space=pltpu.MemorySpace.HBM)
    anywhere = pl.BlockSpec(memory_space=pl.ANY)
    vmem = pl.BlockSpec(memory_space=pltpu.VMEM)
    field, fields = pl.pallas_call(
        body,
        out_shape=(
            jax.ShapeDtypeStruct((V, XS, 128), F32),
            jax.ShapeDtypeStruct((NM, XS, 128), F32),
        ),
        in_specs=[hbm] * 3 + [pl.BlockSpec(memory_space=pltpu.SMEM)] + [hbm] * 3,
        out_specs=(anywhere, vmem),
        scratch_shapes=scratch,
        name="solve",
        compiler_params=pltpu.CompilerParams(
            collective_id=0, has_side_effects=True, vmem_limit_bytes=48 * 2**20
        ),
    )(
        *(
            a if a is octant else pltpu.with_memory_space_constraint(a, pltpu.MemorySpace.HBM)
            for a in (distribution, speeds, weights.reshape(1, V), octant, inverses, inflow, solid_cells)
        )
    )
    parts = 4

    def store(a, b, out_a, out_b, sems):
        copies = [pltpu.make_async_copy(b, out_b, sems.at[parts])]
        for i in range(parts):
            some = pl.ds(i * (V // parts), V // parts)
            copies.append(pltpu.make_async_copy(a.at[some], out_a.at[some], sems.at[i]))
        for copy in copies:
            copy.start()
        for copy in copies:
            copy.wait()

    return pl.pallas_call(
        store,
        out_shape=(
            jax.ShapeDtypeStruct(field.shape, F32),
            jax.ShapeDtypeStruct(fields.shape, F32),
        ),
        in_specs=[anywhere, anywhere],
        out_specs=(hbm, hbm),
        scratch_shapes=[dma((parts + 1,))],
        name="store",
        compiler_params=pltpu.CompilerParams(vmem_limit_bytes=2**20),
    )(field, fields)


def solution(mesh):
    in_specs = (
        P("vel", "gx", None),
        P(None, "vel"),
        P("vel"),
        P("vel"),
        P(),
        P("vel", None),
        P("gx", None),
    )
    out_specs = (P("vel", "gx", None), P(None, "gx", None))
    return jax.shard_map(
        per_device, mesh=mesh, in_specs=in_specs, out_specs=out_specs, check_vma=False
    )
```

```python
import functools

import jax
import jax.numpy as jnp
from jax import lax
from jax.experimental import pallas as pl
from jax.experimental.pallas import tpu as pltpu
from jax.sharding import PartitionSpec as P


SHAKHOV = 4.0 / 45.0
KNUDSEN_STEP = 0.004
ABSORB = 0.3
SWEEPS = 2
MESH = pl.DeviceIdType.MESH
F32 = jnp.float32
BF16 = jnp.bfloat16

V = 432
H = 216
HP = 224
NC = 12
NM = 8
XS = 16
T = 32
PLANE = 32
ZX = 4
ZS = 8
CHIPS = 4
PARTS = 3


def split(x):
    hi = x.astype(BF16)
    return hi, (x - hi.astype(F32)).astype(BF16)


def dot(a, b):
    return jnp.dot(a, b, preferred_element_type=F32)


def rows_of(ax, ay, az, sx, sy, sz):
    cx, cy, cz = ax * sx, ay * sy, az * sz
    e = cx * cx + cy * cy + cz * cz
    f = e - 2.5
    one = jnp.ones_like(cx)
    phi = [one, cx, cy, cz, e * (2.0 / 3.0) - 1.0, cx * f, cy * f, cz * f]
    psi = [one, 2.0 * cx, 2.0 * cy, 2.0 * cz, e - 1.5, SHAKHOV * cx * f, SHAKHOV * cy * f, SHAKHOV * cz * f]
    return phi, psi


def body(
    dist, speeds_in, weights_in, octant, inverses, inflow, solid,
    out_h, out_m,
    speeds, weights, dx, spd, wall, wdir, inv, infl, sbuf, part0, part, own, rb1, first, rb2, mb, mo,
    b3, a3, at, abc, a32, ks, kc, kp, tsc, t2, gs, hloc, mloc, ebuf, esrc, hin, et, ec, kr, l3, wk, enat, abg,
    dsem, isem, ssend, srecv, rsend, rrecv, gsend, grecv, esend, erecv, osend, orecv, olocal,
):
    vel = lax.axis_index("vel")
    gx = lax.axis_index("gx")
    y = gx // 2
    c = gx % 2
    xi = vel // ZS
    zi = vel % ZS
    owner = (vel % 2) == c
    p = jnp.where(c == 0, y, CHIPS - 1 - y)

    def step_of(row, core):
        return jnp.where(core == 0, row, T - 1 - row)

    def classes_of(g):
        return [(8 * g + i) % NC for i in range(8)]

    def remote(src, dst, ss, rs, tv, tg):
        return pltpu.make_async_remote_copy(
            src_ref=src, dst_ref=dst, send_sem=ss, recv_sem=rs, device_id=(tv, tg), device_id_type=MESH
        )

    def send(src, dst, ss, rs, tv, tg, maybe=True):
        if not maybe:
            remote(src, dst, ss, rs, tv, tg).start()
            return
        here = (tv == vel) & (tg == gx)

        @pl.when(here)
        def _():
            pltpu.make_async_copy(src, dst, rs).start()

        @pl.when(jnp.logical_not(here))
        def _():
            remote(src, dst, ss, rs, tv, tg).start()

    small = [
        pltpu.make_async_copy(speeds_in, speeds, isem.at[2]),
        pltpu.make_async_copy(weights_in, weights, isem.at[3]),
    ]
    for copy in small:
        copy.start()
    for x in range(XS):
        pltpu.make_async_copy(dist.at[:, x, :], dx.at[x], dsem.at[x]).start()
    inv_copy = pltpu.make_async_copy(inverses, inv, isem.at[0])
    inv_copy.start()
    infl_copy = pltpu.make_async_copy(
        inflow.at[pl.ds(pl.multiple_of(c * H, 8), H)], infl.at[pl.ds(0, H)], isem.at[1]
    )
    infl_copy.start()

    barrier = pltpu.get_barrier_semaphore()

    def around(i):
        return lax.rem(zi + ZS // 2 + ((i + 1) // 2) * (2 * (i % 2) - 1) + ZS, ZS)

    def greet(i, _):
        tz = around(i)
        for o in (2, 1, 3, 0):
            tv = lax.rem(xi + o, ZX) * ZS + tz
            for cc in range(2):
                if o:
                    pl.semaphore_signal(barrier, inc=1, device_id=(tv, 2 * y + cc), device_id_type=MESH)
                    continue

                @pl.when(jnp.logical_not((tv == vel) & (cc == c)))
                def _():
                    pl.semaphore_signal(barrier, inc=1, device_id=(tv, 2 * y + cc), device_id_type=MESH)

        return 0

    lax.fori_loop(0, ZS, greet, 0)
    for o in range(1, CHIPS):
        for cc in range(2):
            pl.semaphore_signal(
                barrier, inc=1, device_id=(vel, lax.rem(y + o, CHIPS) * 2 + cc), device_id_type=MESH
            )

    lane = lax.broadcasted_iota(jnp.int32, (1, 512), 1)
    for copy in small:
        copy.wait()
    quadrant = octant[0]
    sy = (1 - 2 * lax.rem(quadrant, 2)).astype(F32)
    sz = (1 - 2 * lax.div(quadrant, 2)).astype(F32)
    spd[...] = jnp.zeros_like(spd)
    spd[0:3, 0:V] = speeds[...]
    spd[3:4, 0:V] = weights[...]
    sp = spd[...]
    sx_all = jnp.where(lane < H, 1.0, -1.0).astype(F32)
    phi, _ = rows_of(sp[0:1], sp[1:2], sp[2:3], sx_all, sy, sz)
    for m in range(NM):
        spd[m : m + 1, :] = phi[m] * sp[3:4]
    hi, lo = split(spd[...])
    wall[...] = jnp.concatenate([hi.astype(F32), lo.astype(F32)], axis=0).astype(BF16)

    for x in range(XS):
        pltpu.make_async_copy(dist.at[:, x, :], dx.at[x], dsem.at[x]).wait()
        hi, lo = split(dx[x])
        r = dot(wall[:, 0:V], jnp.concatenate([hi, lo], axis=1))
        part0[x] = r[0:8, 0:128] + r[8:16, 0:128] + r[0:8, 128:256] + r[8:16, 128:256]

    pl.semaphore_wait(barrier, 2 * PLANE - 1 + 2 * (CHIPS - 1))

    def rs1(i, _):
        tz = around(i)
        for o in range(2):
            tv = (2 * c + o) * ZS + tz
            for far in range(2):
                row = o * ZS + lax.rem(tz + far * (ZS // 2), ZS)
                send(part0.at[row], rb1.at[far, vel], rsend.at[0], rrecv.at[0], tv, 2 * y + tz % 2)
        return 0

    lax.fori_loop(0, ZS, rs1, 0)

    for o in range(1, 2 * CHIPS):
        remote(solid, sbuf.at[gx], ssend, srecv, vel, lax.rem(gx + o, 2 * CHIPS)).start()
    pltpu.make_async_copy(solid, sbuf.at[gx], srecv).start()

    sp = jnp.where(c == 0, sp, pltpu.roll(sp, 512 - H, 1))
    sp = jnp.where(lane < H, sp, 0.0)
    sp = sp[:, 0:256]
    live = (lane < H).astype(F32)[:, 0:256]
    sx = (1 - 2 * c).astype(F32)
    phi, psi = rows_of(sp[0:1], sp[1:2], sp[2:3], sx, sy, sz)
    rate = sp[0:1] / (sp[0:1] + KNUDSEN_STEP)
    for m in range(NM):
        spd[m : m + 1, 0:256] = phi[m] * sp[3:4]
        spd[m : m + 1, 256:512] = psi[m] * ((1.0 - rate) * live)
    wd = spd[:, 0:256]
    ps = spd[:, 256:512]
    hi, lo = split(wd)
    wdir[...] = jnp.concatenate([hi.astype(F32), lo.astype(F32)], axis=0).astype(BF16)
    cls = lax.rem(lax.broadcasted_iota(jnp.int32, (8, 256), 1), NC)
    hi, lo = split(ps)
    hi, lo = hi.astype(F32), lo.astype(F32)
    abc[...] = jnp.broadcast_to(rate, (128, 256)).T[0:HP]
    for g in range(3):
        for i, k in enumerate(classes_of(g)):
            at[8 * i : 8 * i + 8] = jnp.where(cls == k, hi, 0.0)
            at[64 + 8 * i : 72 + 8 * i] = jnp.where(cls == k, lo, 0.0)
            at[128 + 8 * i : 136 + 8 * i] = jnp.where(cls == k, hi, 0.0)
        at[192:256] = jnp.zeros((64, 256), F32)
        table = at[...].T
        table = [table[8 * (3 * i + g) : 8 * (3 * i + g) + 8] for i in range(9)]
        table = jnp.concatenate(table + [jnp.zeros((8, 256), F32)], axis=0)
        a3[g] = table.astype(BF16)
        for i in range(9):
            abg[g, i] = abc[8 * (3 * i + g) : 8 * (3 * i + g) + 8]
    pw = abc[...]
    for _ in range(5):
        pw = pw * pw
    a32[...] = pw
    infl[H:HP] = jnp.zeros((HP - H, 128), F32)
    hloc[:, H:HP, :] = jnp.zeros((T, HP - H, 128), F32)
    infl_copy.wait()

    def powers(t, cur):
        cur = cur * rate
        tsc[t] = cur
        return cur

    lax.fori_loop(0, T, powers, wd)
    hi, lo = split(tsc[...].reshape(T * NM, 256))
    t2[0 : T * NM] = hi
    t2[T * NM : 2 * T * NM] = lo

    def remains(t, cur):
        tsc[T - 1 - t] = cur
        return cur * rate

    lax.fori_loop(0, T, remains, ps)
    late = tsc[...].reshape(T * NM, 256).T
    for d in range(2):
        et[d, 0:256] = late[:, 128 * d : 128 * d + 128]
        et[d, 256:288] = jnp.zeros((32, 128), F32)
    for k in range(NC):
        hi, lo = split(jnp.concatenate([et[d, pl.ds(k, 24, stride=NC), :] for d in range(2)], axis=1))
        ec[k] = jnp.concatenate([hi.astype(F32), lo.astype(F32)], axis=0).astype(BF16)

    def gather(rb, n, k, wait):
        @pl.when(owner)
        def _():
            full = rb.at[pl.ds(0, n)]
            remote(full, full, rsend.at[k], rrecv.at[k], vel, gx).wait_recv()
            own[k - 1] = jnp.sum(rb[...].reshape(n // 8, 8, NM, 128), axis=0).sum(axis=0)

    @pl.when(owner)
    def _():
        remote(rb1, rb1, rsend.at[0], rrecv.at[0], vel, gx).wait_recv()
        for far in range(2):
            first[far] = jnp.sum(rb1[far].reshape(PLANE // 8, 8, NM, 128), axis=0).sum(axis=0)

        def one(i, _):
            tz = lax.rem(zi + ZS + (1 - i % 2) * (i // 2 - 2) + (i % 2) * (1 - i // 2), ZS)
            for o in (2, 1, 3, 0):
                tv = lax.rem(xi + o, ZX) * ZS + tz
                for tc in range(2):
                    for far in range(2):
                        row = xi * ZS + lax.rem(zi + far * (ZS // 2), ZS)
                        at_row = row if tc == 0 else T - 1 - row
                        send(first.at[far], mb.at[0, at_row], gsend.at[0], grecv.at[0], tv, 2 * y + tc, o == 0)
            return 0

        lax.fori_loop(0, 4, one, 0)

    def spread(k, dst):
        @pl.when(owner)
        def _():
            def one(i, _):
                tz = around(i)
                for o in (2, 1, 3, 0):
                    tv = lax.rem(xi + o, ZX) * ZS + tz
                    for tc in range(2):
                        at_row = vel if tc == 0 else T - 1 - vel
                        send(own.at[k - 1], dst.at[at_row], gsend.at[k], grecv.at[k], tv, 2 * y + tc, o == 0)
                return 0

            lax.fori_loop(0, ZS, one, 0)


    inv_copy.wait()
    ii = lax.broadcasted_iota(jnp.int32, (128, 128), 0)
    jj = lax.broadcasted_iota(jnp.int32, (128, 128), 1)
    perm = (ii == jnp.where(lax.rem(quadrant, 2) == 0, jj, 127 - jj)).astype(F32).astype(BF16)
    for n in range(NC // 2):
        parts = split(inv[2 * n : 2 * n + 2].reshape(256, 128))
        for q, w in enumerate(parts):
            u = lax.dot_general(perm, w, (((1,), (1,)), ((), ())), preferred_element_type=F32)
            u = jnp.concatenate([u[:, 0:128], u[:, 128:256]], axis=0).astype(BF16)
            v = dot(u, perm).astype(BF16)
            v = jnp.concatenate([v[0:128], v[128:256]], axis=1)
            cols = slice(256 * n, 256 * n + 256)
            if q == 0:
                b3[0:128, cols] = v
                b3[128:256, cols] = v
            else:
                b3[256:384, cols] = v

    remote(sbuf, sbuf, ssend, srecv, vel, gx).wait_recv()
    for chip in range(CHIPS):
        keep = 1.0 - ABSORB * sbuf[2 * chip : 2 * chip + 2].astype(F32).reshape(4, 8, 128)
        keep = (keep[0] * keep[1]) * (keep[2] * keep[3])
        for s in (4, 2, 1):
            keep = keep * pltpu.roll(keep, s, 0)
        kp[chip] = keep

    def cells(t, cur):
        x = step_of(t, c)
        keep = 1.0 - ABSORB * sbuf[2 * y + x // XS, pl.ds(x % XS, 1), :].astype(F32)
        keep = jnp.broadcast_to(keep, (8, 128))
        cur = cur * keep
        ks[t] = keep
        kc[t] = cur
        return cur

    lax.fori_loop(0, T, cells, jnp.ones((8, 128), F32))

    def left(t, cur):
        kr[T - 1 - t] = cur
        return cur * ks[T - 1 - t]

    lax.fori_loop(0, T, left, jnp.ones((8, 128), F32))

    for s in range(SWEEPS):
        remote(mb.at[s], mb.at[s], gsend.at[s], grecv.at[s], vel, gx).wait_recv()
        hi, lo = split(mb[s].reshape(T * NM, 128))
        l3[...] = jnp.concatenate([hi, lo, hi], axis=1)
        for part_of in range(PARTS):
            for n in range(2 * part_of, 2 * part_of + 2):
                g = dot(l3[...], b3[:, 256 * n : 256 * n + 256]).reshape(T, NM, 256)
                gs[:, 16 * n : 16 * n + 16, :] = jnp.concatenate([g[:, :, 0:128], g[:, :, 128:256]], axis=1)
                for d in range(2):
                    hi, lo = split((g[:, :, 128 * d : 128 * d + 128] * kr[...]).reshape(T * NM, 128))
                    wk[2 * n + d] = jnp.concatenate([hi, lo], axis=1)
            for d in range(4):
                r = dot(ec[4 * part_of + d], wk[4 * part_of + d])
                r = r[0:24, 0:128] + r[24:48, 0:128] + r[0:24, 128:256]
                esrc[s, part_of, pl.ds(d, H // NC, stride=4), :] = r[0 : H // NC]

            for gap in (2, 1, 3):
                q = p + gap

                @pl.when(q < CHIPS)
                def _():
                    ty = jnp.where(c == 0, q, CHIPS - 1 - q)
                    remote(
                        esrc.at[s, part_of], ebuf.at[s, p, part_of], esend.at[s, gap - 1], erecv.at[s, p],
                        vel, 2 * ty + c,
                    ).start()

        def march(u, h):
            t = 2 * u
            hi, lo = split(jnp.concatenate([gs[t], gs[t + 1]], axis=1))
            after = []
            for g in range(3):
                pairs = [k // 2 for k in classes_of(g)[::2]]
                hs = [hi[16 * n : 16 * n + 16] for n in pairs]
                ls = [lo[16 * n : 16 * n + 16] for n in pairs]
                r = dot(a3[g, :, 0:192], jnp.concatenate(hs + hs + ls, axis=0))
                now = h[g]
                for d in range(2):
                    now = now * (abg[g] * ks[t + d][None]) + r[0:72, 128 * d : 128 * d + 128].reshape(9, 8, 128)
                    for i in range(9):
                        hloc[t + d, 8 * (3 * i + g) : 8 * (3 * i + g) + 8, :] = now[i]
                after.append(now)
            return tuple(after)

        lax.fori_loop(0, T // 2, march, (jnp.zeros((9, 8, 128), F32),) * 3, unroll=8)

        def local_moments(u, _):
            t = 2 * u
            hi, lo = split(jnp.concatenate([hloc[t], hloc[t + 1]], axis=1))
            r = dot(wdir[:, 0:HP], hi) + dot(wdir[:, 0:HP], lo)
            r = r[0:8] + r[8:16]
            mloc[t] = r[:, 0:128]
            mloc[t + 1] = r[:, 128:256]
            return 0

        lax.fori_loop(0, T // 2, local_moments, 0, unroll=8)

        hin[...] = infl[...]
        for q in range(CHIPS - 1):

            @pl.when(q < p)
            def _():
                full = ebuf.at[s, q]
                remote(full, full, esend.at[s, 0], erecv.at[s, q], vel, gx).wait_recv()
                k = kp[jnp.where(c == 0, q, CHIPS - 1 - q)]
                span = a32[...].reshape(HP // 8, 8, 128) * k[None]
                now = hin[...].reshape(HP // 8, 8, 128) * span
                for k in range(NC):
                    own_rows = pl.ds(k, H // NC, stride=NC)
                    enat[own_rows, :] = ebuf[s, q, k // 4, pl.ds(k % 4, H // NC, stride=4), :]
                now = now[0 : H // 8] + enat[...].reshape(H // 8, 8, 128)
                hin[0:H] = now.reshape(H, 128)

        hi, lo = split(hin[...])
        r = dot(t2[:, 0:HP], jnp.concatenate([hi, lo], axis=1))
        n = T * NM
        r = (r[0:n, 0:128] + r[n : 2 * n, 0:128]) + (r[0:n, 128:256] + r[n : 2 * n, 128:256])
        part[s] = mloc[...] + kc[...] * r.reshape(T, NM, 128)

        def rs(i, _):
            tz = around(i)
            for o in (2, 1, 3, 0):
                row = lax.rem(xi + o, ZX) * ZS + tz
                send(
                    part.at[s, step_of(row, c)], rb2.at[s, 2 * vel + c], rsend.at[s + 1], rrecv.at[s + 1],
                    row, 2 * y + tz % 2, o == 0,
                )
            return 0

        lax.fori_loop(0, ZS, rs, 0)

        if s == SWEEPS - 1:
            def finish(t, h):
                a = abc[...].reshape(HP // 8, 8, 128)
                h = h * (a * ks[t][None])
                hloc[t] = (hloc[t].reshape(HP // 8, 8, 128) + h).reshape(HP, 128)
                return h

            start = pl.multiple_of(c * H, 8)

            def far(t, h):
                h = finish(t, h)
                x = jnp.where(c == 0, t - XS, T - 1 - t)
                remote(
                    hloc.at[t, pl.ds(0, H)], out_h.at[pl.ds(start, H), x, :], osend, orecv, vel, 2 * y + 1 - c
                ).start()
                return h

            def near(t, h):
                h = finish(t, h)
                x = jnp.where(c == 0, t, XS - 1 - t)
                pltpu.make_async_copy(hloc.at[t, pl.ds(0, H)], out_h.at[pl.ds(start, H), x, :], olocal).start()
                return h

            h = lax.fori_loop(0, XS, near, hin[...].reshape(HP // 8, 8, 128))
            lax.fori_loop(XS, T, far, h)

        gather(rb2.at[s], 2 * PLANE, s + 1, None)
        if s < SWEEPS - 1:
            spread(s + 1, mb.at[s + 1])

    last = SWEEPS
    section = vel // XS

    @pl.when(owner)
    def _():
        def one(i, _):
            tz = around(i)
            for o in (2, 1, 3, 0):
                tv = lax.rem(xi + o, ZX) * ZS + tz
                send(own.at[last - 1], mo.at[vel % XS], gsend.at[last], grecv.at[last], tv, 2 * y + section, o == 0)
            return 0

        lax.fori_loop(0, ZS, one, 0)

    remote(mo, mo, gsend.at[last], grecv.at[last], vel, gx).wait_recv()
    for x in range(XS):
        out_m[:, x, :] = mo[x]

    for o in range(1, 2 * CHIPS):
        remote(solid, sbuf.at[gx], ssend, srecv, vel, gx).wait_send()
    mine = owner & (section == c)

    def drain(buf, n, less, sem, by=1):
        @pl.when(less)
        def _():
            remote(buf.at[pl.ds(0, n - by)], buf.at[pl.ds(0, n - by)], sem, sem, vel, gx).wait_send()

        @pl.when(jnp.logical_not(less))
        def _():
            remote(buf.at[pl.ds(0, n)], buf.at[pl.ds(0, n)], sem, sem, vel, gx).wait_send()

    drain(rb1.at[0], 2 * XS, mine, rsend.at[0], 2)
    for s in range(SWEEPS):
        drain(part.at[s], T, owner, rsend.at[s + 1])
        for gap in (2, 1, 3):

            @pl.when(p + gap < CHIPS)
            def _():
                remote(esrc.at[s], esrc.at[s], esend.at[s, gap - 1], esend.at[s, gap - 1], vel, gx).wait_send()

    @pl.when(owner)
    def _():
        for k in range(SWEEPS):
            few = rb2.at[0, pl.ds(0, 2 * PLANE - (2 if k == 0 else 1))]
            remote(few, few, gsend.at[k], gsend.at[k], vel, gx).wait_send()
        drain(rb2.at[0], PLANE, section == c, gsend.at[last])

    half = hloc.at[pl.ds(0, XS), pl.ds(0, H)]
    remote(half, half, osend, orecv, vel, gx).wait()
    pltpu.make_async_copy(half, half, olocal).wait()


def per_device(distribution, speeds, weights, octant, inverses, inflow, solid_cells):
    dma = pltpu.SemaphoreType.DMA
    vm = pltpu.VMEM
    scratch = [
        vm((3, V), F32), vm((1, V), F32),
        vm((XS, V, 128), F32), vm((8, 512), F32), vm((16, 512), BF16), vm((16, 256), BF16),
        vm((NC, 128, 128), F32), vm((HP, 128), F32), vm((2 * CHIPS, XS, 128), jnp.int32),
        vm((XS, NM, 128), F32), vm((SWEEPS, T, NM, 128), F32), vm((SWEEPS, NM, 128), F32),
        vm((2, PLANE, NM, 128), F32), vm((2, NM, 128), F32), vm((SWEEPS, 2 * PLANE, NM, 128), F32), vm((SWEEPS, T, NM, 128), F32),
        vm((XS, NM, 128), F32),
        vm((384, NC * 128), BF16), vm((3, 80, 256), BF16), vm((256, 256), F32), vm((HP, 128), F32),
        vm((HP, 128), F32), vm((T, 8, 128), F32), vm((T, 8, 128), F32), vm((CHIPS, 8, 128), F32),
        vm((T, 8, 256), F32), vm((2 * T * NM, 256), BF16), vm((T, 96, 128), F32), vm((T, HP, 128), F32),
        vm((T, NM, 128), F32), vm((SWEEPS, CHIPS - 1, PARTS, H // PARTS, 128), F32),
        vm((SWEEPS, PARTS, H // PARTS, 128), F32),
        vm((HP, 128), F32), vm((2, 288, 128), F32), vm((NC, 48, 256), BF16), vm((T, 8, 128), F32),
        vm((T * NM, 384), BF16), vm((NC, T * NM, 256), BF16), vm((H, 128), F32), vm((3, 9, 8, 128), F32),
        dma((XS,)), dma((4,)), dma, dma, dma((SWEEPS + 1,)), dma((SWEEPS + 1,)), dma((SWEEPS + 1,)),
        dma((SWEEPS + 1,)), dma((SWEEPS, CHIPS - 1)), dma((SWEEPS, CHIPS - 1)), dma, dma, dma,
    ]
    hbm = pl.BlockSpec(memory_space=pltpu.MemorySpace.HBM)
    anywhere = pl.BlockSpec(memory_space=pl.ANY)
    vmem = pl.BlockSpec(memory_space=pltpu.VMEM)
    field, fields = pl.pallas_call(
        body,
        out_shape=(
            jax.ShapeDtypeStruct((V, XS, 128), F32),
            jax.ShapeDtypeStruct((NM, XS, 128), F32),
        ),
        in_specs=[hbm] * 3 + [pl.BlockSpec(memory_space=pltpu.SMEM)] + [hbm] * 3,
        out_specs=(anywhere, vmem),
        scratch_shapes=scratch,
        name="solve",
        compiler_params=pltpu.CompilerParams(
            collective_id=0, has_side_effects=True, vmem_limit_bytes=48 * 2**20
        ),
    )(
        *(
            a if a is octant else pltpu.with_memory_space_constraint(a, pltpu.MemorySpace.HBM)
            for a in (distribution, speeds, weights.reshape(1, V), octant, inverses, inflow, solid_cells)
        )
    )
    parts = 4

    def store(a, b, out_a, out_b, sems):
        copies = [pltpu.make_async_copy(b, out_b, sems.at[parts])]
        for i in range(parts):
            some = pl.ds(i * (V // parts), V // parts)
            copies.append(pltpu.make_async_copy(a.at[some], out_a.at[some], sems.at[i]))
        for copy in copies:
            copy.start()
        for copy in copies:
            copy.wait()

    return pl.pallas_call(
        store,
        out_shape=(
            jax.ShapeDtypeStruct(field.shape, F32),
            jax.ShapeDtypeStruct(fields.shape, F32),
        ),
        in_specs=[anywhere, anywhere],
        out_specs=(hbm, hbm),
        scratch_shapes=[dma((parts + 1,))],
        name="store",
        compiler_params=pltpu.CompilerParams(vmem_limit_bytes=2**20),
    )(field, fields)


def solution(mesh):
    in_specs = (
        P("vel", "gx", None),
        P(None, "vel"),
        P("vel"),
        P("vel"),
        P(),
        P("vel", None),
        P("gx", None),
    )
    out_specs = (P("vel", "gx", None), P(None, "gx", None))
    return jax.shard_map(
        per_device, mesh=mesh, in_specs=in_specs, out_specs=out_specs, check_vma=False
    )
```
